256 devices in a mesh: cube: 8 (over z_lo, core), row: 8 (over z_hi, x), col: 4 (over y).
Axes of the slice: x: 4, y: 4, z: 8 (z_hi: 2, z_lo: 4; z = z_hi * 4 + z_lo), core: 2. Of those that a mesh axis runs over, the one named last changes fastest.
Arguments:
- child_front: float32 [8, 12, 8, 2, 8, 12, 4, 128], P('cube', None, 'row', None, None, None, 'col'), may hold values from -6 to 25, as said below
- parent_front: float32 [12, 8, 8, 8, 12, 4, 128], P(None, 'row', 'cube', None, None, 'col'), may hold values from -6 to 25, as said below
- border_map: int32 [2, 11], replicated, may hold values from 0 to 11, as said below
Outputs:
- child_factor: float32 [8, 12, 8, 2, 8, 1, 4, 128], P('cube', None, 'row', None, None, None, 'col')
- parent_factor: float32 [12, 8, 8, 8, 1, 4, 128], P(None, 'row', 'cube', None, None, 'col')
- parent_update: float32 [11, 8, 8, 8, 11, 4, 128], P(None, 'row', 'cube', None, None, 'col')
The draws below stay inside these ranges and needn't reach their ends.
Inputs may be any that keep to these rules, and one draw needn't show every extreme that they name: `child_front`: each C_c, read through the stated layout, is symmetric positive definite. `parent_front`: read as a matrix in natural order, the parent front is symmetric positive definite. `border_map`: each row lists 11 different parent blocks in increasing order.
All inputs are finite; a program needn't handle non-finite values.
Results may differ from the reference program's by a relative error of at most 0.00011.
Values sent between devices are 32-bit elements; how exact they have to be, the bound alone decides.
A program may use at most 64 MiB of HBM per device.

```python
import jax
import jax.numpy as jnp
from jax import lax

PANEL = 512
CHILD_FRONT = 6144
PARENT_FRONT = 6144
CHILD_PANELS = 1
PARENT_PANELS = 1
CHILDREN = 2
HALF = 4
CHILD_CYCLES = 12
PARENT_CYCLES = 12
BORDER_CYCLES = 11
TAIL_CYCLES = 11
SUB_ROWS = 8
COL_BLOCK = 128
N_CUBE = 8
N_ROW = 8
N_COL = 4


def definite_front(key, order):
    keys = jax.random.split(key, 2)
    raw = jax.random.truncated_normal(keys[0], -4.0, 4.0, (order, order), jnp.float32)
    gram = jnp.dot(raw, raw.T, precision=lax.Precision.HIGHEST) / order
    diagonal = jax.random.uniform(keys[1], (order,), jnp.float32, 0.05, 0.25)
    matrix = gram + jnp.diag(diagonal)
    return 0.5 * (matrix + matrix.T)


def draw_child_front(key, part):

    def one_child(index):
        return definite_front(jax.random.fold_in(key, index), CHILD_FRONT)
    fronts = lax.map(one_child, jnp.arange(CHILDREN))
    laid = fronts.reshape(CHILDREN, CHILD_CYCLES, N_ROW, CHILDREN, HALF, SUB_ROWS, CHILD_CYCLES, N_COL, COL_BLOCK)
    laid = laid.transpose(0, 4, 1, 2, 3, 5, 6, 7, 8)
    return laid.reshape(N_CUBE, CHILD_CYCLES, N_ROW, CHILDREN, SUB_ROWS, CHILD_CYCLES, N_COL, COL_BLOCK)


def draw_parent_front(key, part):
    matrix = definite_front(jax.random.fold_in(key, 1001), PARENT_FRONT)
    return matrix.reshape(PARENT_CYCLES, N_ROW, N_CUBE, SUB_ROWS, PARENT_CYCLES, N_COL, COL_BLOCK)


def draw_border_map(key, part):

    def choose(index):
        shuffled = jax.random.permutation(jax.random.fold_in(key, 2002 + index), PARENT_CYCLES)
        return jnp.sort(shuffled[:BORDER_CYCLES]).astype(jnp.int32)
    return jax.vmap(choose)(jnp.arange(CHILDREN))


def setup_inputs(seed: int = 0) -> dict:
    splits = jax.random.split(jax.random.key(seed), 4)
    return {
        "child_front": draw_child_front(jax.random.fold_in(splits[3], 71), 0),
        "parent_front": draw_parent_front(jax.random.fold_in(splits[3], 71), 0),
        "border_map": draw_border_map(jax.random.fold_in(splits[3], 71), 0),
    }


HIGHEST = lax.Precision.HIGHEST

def partial_factor(matrix, panels):
    columns = []
    for panel in range(panels):
        start = panel * PANEL
        finish = start + PANEL
        lower = jnp.linalg.cholesky(matrix[start:finish, start:finish])
        inverse = jax.scipy.linalg.solve_triangular(lower, jnp.eye(PANEL, dtype=matrix.dtype), lower=True)
        factor = jnp.dot(matrix[start:, start:finish], inverse.T, precision=HIGHEST)
        across = jnp.dot(inverse, matrix[start:finish, finish:], precision=HIGHEST)
        matrix = matrix.at[finish:, finish:].add(-jnp.dot(factor[PANEL:], across, precision=HIGHEST))
        columns.append(jnp.concatenate([jnp.zeros((start, PANEL), matrix.dtype), factor], 0))
    return (jnp.concatenate(columns, 1), matrix)

def reference(child_front, parent_front, border_map):
    offsets = jnp.arange(PANEL, dtype=jnp.int32)
    assembled = parent_front.reshape(PARENT_FRONT, PARENT_FRONT)
    halves = child_front.reshape(CHILDREN, HALF, CHILD_CYCLES, N_ROW, CHILDREN, SUB_ROWS, CHILD_CYCLES, N_COL, COL_BLOCK)
    factors = []
    for child in range(CHILDREN):
        matrix = halves[child].transpose(1, 2, 3, 0, 4, 5, 6, 7).reshape(CHILD_FRONT, CHILD_FRONT)
        factor, updated = partial_factor(matrix, CHILD_PANELS)
        laid = factor.reshape(CHILD_CYCLES, N_ROW, CHILDREN, HALF, SUB_ROWS, CHILD_PANELS, N_COL, COL_BLOCK)
        factors.append(laid.transpose(3, 0, 1, 2, 4, 5, 6, 7))
        border = updated[CHILD_PANELS * PANEL:, CHILD_PANELS * PANEL:]
        places = (border_map[child].astype(jnp.int32)[:, None] * PANEL + offsets[None, :]).reshape(-1).astype(jnp.int32)
        assembled = assembled.at[places[:, None], places[None, :]].add(border)
    child_factor = jnp.stack(factors, 0).reshape(N_CUBE, CHILD_CYCLES, N_ROW, CHILDREN, SUB_ROWS, CHILD_PANELS, N_COL, COL_BLOCK)
    parent_factor, updated = partial_factor(assembled, PARENT_PANELS)
    tail = updated[PARENT_PANELS * PANEL:, PARENT_PANELS * PANEL:]
    return (child_factor, parent_factor.reshape(PARENT_CYCLES, N_ROW, N_CUBE, SUB_ROWS, PARENT_PANELS, N_COL, COL_BLOCK), tail.reshape(TAIL_CYCLES, N_ROW, N_CUBE, SUB_ROWS, TAIL_CYCLES, N_COL, COL_BLOCK))
```

```python
import functools

import jax
import jax.numpy as jnp
from jax import lax
from jax.experimental import pallas as pl
from jax.experimental.pallas import tpu as pltpu
from jax.sharding import PartitionSpec as P

CHILD_PANELS = 1
PARENT_PANELS = 1
CHILDREN = 2


HIGHEST = lax.Precision.HIGHEST
HI = HIGHEST
NB=128

def base(T, out_ref, w):
    rows = list(T)
    lane = lax.broadcasted_iota(jnp.int32, (8, NB), 1)
    sub = lax.broadcasted_iota(jnp.int32, (8, NB), 0)
    n = NB // 8
    bc_lane = lambda x, j: jnp.broadcast_to(x[:, j:j+1], (8, NB))
    bc_sub = lambda x, s: jnp.broadcast_to(x[s:s+1, :], (8, NB))
    for j in range(0, NB, w):
        t, s = j // 8, j % 8
        c = [{i: bc_lane(rows[i], j + a) for i in range(t, n)} for a in range(w)]
        inblk = (lane >= j) & (lane < j + w)
        r = []
        for a in range(w):
            x = bc_sub(rows[t], s + a)
            x = jnp.where(lane == j + a, 1.0, jnp.where(inblk, 0.0, x) if w > 1 else x)
            r.append(x)
        pv = {(a, b): bc_sub(c[b][t], s + a) for a in range(w) for b in range(a, w)}
        z = []
        for a in range(w):
            inv = 1.0 / pv[a, a]
            rs = lax.rsqrt(pv[a, a])
            za = r[a] * inv
            z.append(za)
            row = jnp.where(lane <= j + a, r[a] * rs, 0.0)
            out_ref[j + a:j + a + 1, :] = row[:1, :]
            for b in range(a + 1, w):
                m = pv[a, b] * inv
                r[b] = r[b] - pv[a, b] * za
                for d in range(b, w):
                    pv[b, d] = pv[b, d] - m * pv[a, d]
                for i in range(t, n):
                    c[b][i] = c[b][i] - c[a][i] * m
        for i in range(t, n):
            if i == t and s + w == 8:
                continue
            acc = jnp.where(inblk, 0.0, rows[i])
            for a in range(w):
                acc = acc - c[a][i] * z[a]
            rows[i] = acc if i > t else jnp.where(sub >= s + w, acc, rows[i])

def chol_inv(B, Vd, w, n=512):
    nk = n // NB
    for k in range(nk):
        kb = slice(k*NB, (k+1)*NB)
        T = [B[k*NB+8*i:k*NB+8*i+8, kb] for i in range(NB//8)]
        base(T, Vd, w)
        V = Vd[...]
        if k + 1 < nk:
            rest = slice((k+1)*NB, n)
            L = lax.dot_general(B[rest, kb], V, (((1,), (1,)), ((), ())), precision=HI, preferred_element_type=jnp.float32)
            R2 = jnp.dot(V, B[kb, rest], precision=HI, preferred_element_type=jnp.float32)
        if k:
            left = slice(0, k*NB)
            R1 = jnp.dot(V, B[kb, left], precision=HI, preferred_element_type=jnp.float32)
            B[kb, left] = R1
        B[kb, kb] = V
        if k + 1 < nk:
            if k:
                B[rest, left] = B[rest, left] - jnp.dot(L, R1, precision=HI, preferred_element_type=jnp.float32)
            B[rest, kb] = -jnp.dot(L, V, precision=HI, preferred_element_type=jnp.float32)
            B[rest, rest] = B[rest, rest] - jnp.dot(L, R2, precision=HI, preferred_element_type=jnp.float32)
            B[kb, rest] = jnp.zeros((NB, n-(k+1)*NB), jnp.float32)

def kern(w, a, o, B, Vd):
    B[...] = a[...]
    chol_inv(B, Vd, w)
    o[...] = B[...]


def partner(block, axis, bit):
    count = lax.axis_size(axis)
    route = []
    for low in range(count):
        high = low | 1 << bit
        if high != low and high < count:
            route += [(low, high), (high, low)]
    return lax.ppermute(block, axis, route)


def lower_inverse(diagonal):
    return pl.pallas_call(
        functools.partial(kern, 8),
        out_shape=jax.ShapeDtypeStruct(diagonal.shape, jnp.float32),
        in_specs=[pl.BlockSpec(memory_space=pltpu.VMEM)],
        out_specs=pl.BlockSpec(memory_space=pltpu.VMEM),
        scratch_shapes=[pltpu.VMEM(diagonal.shape, jnp.float32), pltpu.VMEM((NB, NB), jnp.float32)],
        name="inverse_factor",
    )(diagonal)


def own_columns(factor, col_block, start_rows):
    mine = lax.dynamic_slice_in_dim(factor, lax.axis_index("col") * col_block, col_block, 1)
    return jnp.concatenate([jnp.zeros((start_rows, col_block), factor.dtype), mine], 0)


def shards(child_front, parent_front, border_map):
    n_row = lax.axis_size("row")
    n_col = lax.axis_size("col")
    n_cube = lax.axis_size("cube")
    half = n_cube // CHILDREN
    child = lax.axis_index("cube") // half
    child_cycles = child_front.shape[1]
    sub_rows = child_front.shape[4]
    col_block = child_front.shape[7]
    block_rows = CHILDREN * sub_rows
    width = col_block * n_col
    natural_shape = (n_row, CHILDREN, half, sub_rows)
    front = child_front.reshape(child_cycles * block_rows, child_cycles * col_block)
    panel = 0
    row_start = panel * block_rows
    row_end = row_start + block_rows
    col_start = panel * col_block
    col_end = col_start + col_block
    top = front[row_start:row_end, col_start:]
    span = top.shape[1]
    piece = top[None]
    for bit in range(half.bit_length() - 1):
        other = partner(piece, "cube", bit)
        upper = lax.axis_index("cube") // 2**bit % 2 == 1
        piece = jnp.where(
            upper, jnp.concatenate([other, piece], 0), jnp.concatenate([piece, other], 0)
        )
    rows_whole = lax.all_gather(piece[None], "row", axis=0, tiled=True).reshape(width, span)
    gathered_shape = (n_row, half, CHILDREN, sub_rows)
    to_natural = (0, 2, 1, 3)
    to_gathered = (0, 2, 1, 3)
    corner_rows = rows_whole[:, :col_block].reshape(gathered_shape + (col_block,))
    corner_rows = corner_rows.transpose(to_natural + (4,)).reshape(width, col_block)
    corner = lax.all_gather(corner_rows, "col", axis=1, tiled=True)
    cols_whole = lax.all_gather(front[row_start:, col_start:col_end], "col", axis=1, tiled=True)
    inverse = lower_inverse(corner)
    mixing = (
        inverse.reshape((width,) + natural_shape)
        .transpose((0,) + tuple((1 + k for k in to_gathered)))
        .reshape(width, width)
    )
    factor = jnp.dot(cols_whole, inverse.T, precision=HIGHEST)
    across = jnp.dot(mixing, rows_whole, precision=HIGHEST)
    front = front.at[row_end:, col_end:].add(
        -jnp.dot(factor[block_rows:], across[:, col_block:], precision=HIGHEST)
    )
    child_columns = own_columns(factor, col_block, row_start)
    child_factor = child_columns.reshape(
        1, child_cycles, 1, CHILDREN, sub_rows, CHILD_PANELS, 1, col_block
    )
    parent_cycles = parent_front.shape[0]
    border_cycles = child_cycles - CHILD_PANELS
    border = front[CHILD_PANELS * block_rows :, CHILD_PANELS * col_block :]
    blocks = border.reshape(border_cycles, CHILDREN, sub_rows, border_cycles, col_block)
    kept = lax.dynamic_index_in_dim(blocks, child, 1, keepdims=False)
    sent = lax.dynamic_index_in_dim(blocks, 1 - child, 1, keepdims=False)
    received = partner(sent, "cube", half.bit_length() - 1)
    own_map = lax.dynamic_index_in_dim(border_map, child, 0, keepdims=False)
    sibling_map = lax.dynamic_index_in_dim(border_map, 1 - child, 0, keepdims=False)
    targets = jnp.arange(parent_cycles, dtype=jnp.int32)
    select = (jnp.stack([own_map, sibling_map], 0)[:, :, None] == targets[None, None, :]).astype(
        jnp.float32
    )
    contributions = jnp.stack([kept, received], 0)
    placed = jnp.einsum("cip,ciajb,cjq->paqb", select, contributions, select, precision=HIGHEST)
    assembled = parent_front.reshape(parent_cycles * sub_rows, parent_cycles * col_block)
    assembled = assembled + placed.reshape(parent_cycles * sub_rows, parent_cycles * col_block)
    panel = 0
    row_start = panel * sub_rows
    row_end = row_start + sub_rows
    col_start = panel * col_block
    col_end = col_start + col_block
    corner = assembled[row_start:row_end, col_start:col_end]
    pieces = lax.all_gather(corner[None], ("cube", "row", "col"), axis=0, tiled=True)
    diagonal = (
        pieces.reshape(n_cube, n_row, n_col, sub_rows, col_block)
        .transpose(1, 0, 3, 2, 4)
        .reshape(width, width)
    )
    inverse = lower_inverse(diagonal)
    top = assembled[row_start:row_end, col_start:]
    partial_rows = lax.all_gather(top[None, None], "cube", axis=1, tiled=True)
    sectioned = lax.all_gather(partial_rows, "row", axis=0, tiled=True)
    rows_whole = sectioned.reshape(width, top.shape[1])
    cols_whole = lax.all_gather(assembled[row_start:, col_start:col_end], "col", axis=1, tiled=True)
    factor = jnp.dot(cols_whole, inverse.T, precision=HIGHEST)
    across = jnp.dot(inverse, rows_whole, precision=HIGHEST)
    assembled = assembled.at[row_end:, col_end:].add(
        -jnp.dot(factor[sub_rows:], across[:, col_block:], precision=HIGHEST)
    )
    parent_columns = own_columns(factor, col_block, row_start)
    parent_factor = parent_columns.reshape(
        parent_cycles, 1, 1, sub_rows, PARENT_PANELS, 1, col_block
    )
    tail_cycles = parent_cycles - PARENT_PANELS
    tail = assembled[PARENT_PANELS * sub_rows :, PARENT_PANELS * col_block :]
    parent_update = tail.reshape(tail_cycles, 1, 1, sub_rows, tail_cycles, 1, col_block)
    return (child_factor, parent_factor, parent_update)


def solution(mesh):
    return jax.shard_map(
        shards,
        mesh=mesh,
        in_specs=(
            P("cube", None, "row", None, None, None, "col", None),
            P(None, "row", "cube", None, None, "col", None),
            P(),
        ),
        out_specs=(
            P("cube", None, "row", None, None, None, "col", None),
            P(None, "row", "cube", None, None, "col", None),
            P(None, "row", "cube", None, None, "col", None),
        ),
        check_vma=False,
    )
```

```python
import functools

import jax
import jax.numpy as jnp
from jax import lax
from jax.experimental import pallas as pl
from jax.experimental.pallas import tpu as pltpu
from jax.sharding import PartitionSpec as P

CHILDREN = 2
SUB = 8
LANE = 128
WIDTH = 512
STEP = 8
HIGHEST = lax.Precision.HIGHEST
MESH = pl.DeviceIdType.MESH
F32 = jnp.float32


def mm(a, b):
    return jnp.dot(a, b, precision=HIGHEST, preferred_element_type=F32)


def mm_t(a, b):
    return lax.dot_general(
        a, b, (((1,), (1,)), ((), ())), precision=HIGHEST, preferred_element_type=F32
    )


def diagonal_inverse(tiles, out_ref):
    rows = list(tiles)
    lane = lax.broadcasted_iota(jnp.int32, (SUB, LANE), 1)
    n = LANE // SUB
    for t in range(n):
        j = t * SUB
        column = [
            {i: jnp.broadcast_to(rows[i][:, j + a : j + a + 1], (SUB, LANE)) for i in range(t, n)}
            for a in range(STEP)
        ]
        inside = (lane >= j) & (lane < j + STEP)
        right = []
        for a in range(STEP):
            row = jnp.broadcast_to(rows[t][a : a + 1, :], (SUB, LANE))
            right.append(jnp.where(lane == j + a, 1.0, jnp.where(inside, 0.0, row)))
        pivot = {
            (a, b): jnp.broadcast_to(column[b][t][a : a + 1, :], (SUB, LANE))
            for a in range(STEP)
            for b in range(a, STEP)
        }
        scaled = []
        for a in range(STEP):
            inverse = 1.0 / pivot[a, a]
            scaled.append(right[a] * inverse)
            row = jnp.where(lane <= j + a, right[a] * lax.rsqrt(pivot[a, a]), 0.0)
            out_ref[j + a : j + a + 1, :] = row[:1, :]
            for b in range(a + 1, STEP):
                ratio = pivot[a, b] * inverse
                right[b] = right[b] - pivot[a, b] * scaled[a]
                for d in range(b, STEP):
                    pivot[b, d] = pivot[b, d] - ratio * pivot[a, d]
                for i in range(t + 1, n):
                    column[b][i] = column[b][i] - column[a][i] * ratio
        for i in range(t + 1, n):
            rest = jnp.where(inside, 0.0, rows[i])
            for a in range(STEP):
                rest = rest - column[a][i] * scaled[a]
            rows[i] = rest


def inverse_factor(matrix, block, strip, hook):
    blocks = WIDTH // LANE

    def body(k, carry):
        here = pl.ds(pl.multiple_of(k * LANE, LANE), LANE)
        tiles = [
            matrix[pl.ds(pl.multiple_of(k * LANE + SUB * i, SUB), SUB), here]
            for i in range(LANE // SUB)
        ]
        diagonal_inverse(tiles, block)
        hook(k)
        strip[...] = mm(block[...], matrix[here, :])
        strip[:, here] = block[...]
        for i in range(1, blocks):
            below = slice(i * LANE, (i + 1) * LANE)

            @pl.when(k < i)
            def _():
                left = mm_t(matrix[below, here], block[...])
                matrix[below, here] = jnp.zeros((LANE, LANE), F32)
                matrix[below, :] = matrix[below, :] - mm(left, strip[...])

        for i in range(blocks):
            columns = slice(i * LANE, (i + 1) * LANE)
            matrix[here, columns] = jnp.where(k >= i, strip[:, columns], 0.0)
        return carry

    lax.fori_loop(0, blocks, body, 0)


def place():
    cube, row, col = lax.axis_index("cube"), lax.axis_index("row"), lax.axis_index("col")
    return cube, row, col


class Sends:
    def __init__(self, send, recv):
        self.send, self.recv, self.copies = send, recv, []

    def add(self, src, dst, device):
        index = len(self.copies)
        copy = pltpu.make_async_remote_copy(
            src_ref=src,
            dst_ref=dst,
            send_sem=self.send.at[index],
            recv_sem=self.recv.at[index],
            device_id=device,
            device_id_type=MESH,
        )
        self.copies.append(copy)

    def start(self):
        for copy in self.copies:
            copy.start()

    def arrived(self):
        for copy in self.copies:
            copy.wait_recv()

    def left(self):
        for copy in self.copies:
            copy.wait_send()


def greet(peers):
    barrier = pltpu.get_barrier_semaphore()
    for device in peers:
        pl.semaphore_signal(barrier, inc=1, device_id=device, device_id_type=MESH)
    pl.semaphore_wait(barrier, len(peers))


def child_kernel(
    front, factor, update,
    panel, corner, across, matrix, block, strip, wide, whole, local,
    s_y, r_y, s_rest, r_rest, s_dz, r_dz, s_dx, r_dx, s_dc, r_dc, s_az, r_az, s_ax, r_ax, s_ac, r_ac,
):
    cube, row, col = place()
    core, zl, child = cube % 2, cube // 2 % 2, cube // 4
    x, zh = row % 4, row // 4
    cycles = front.shape[0]
    ys = [(cube, row, (col + d) % 4) for d in (1, 2, 3)]
    zs = [
        (child * 4 + (zl + d % 2) % 2 * 2 + core, (zh + d // 2) % 2 * 4 + x, col) for d in (1, 2, 3)
    ]
    xs = [(cube, zh * 4 + (x + d) % 4, col) for d in (1, 2, 3)]
    other = (cube + 1 - 2 * core, row, col)
    greet(ys + zs + xs + [other])

    first, rest = Sends(s_y, r_y), Sends(s_rest, r_rest)
    for device in ys:
        first.add(front.at[0, :, :, 0:LANE], panel.at[col, 0], device)
    for device in ys:
        rest.add(front.at[1:, :, :, 0:LANE], panel.at[col, 1:], device)
    first.start()
    own = pltpu.make_async_copy(front.at[:, :, :, 0:LANE], panel.at[col], local.at[0])
    own.start()
    mine = pltpu.make_async_copy(
        front.at[0, :, :, LANE:], across.at[zh, x, :, zl, core], local.at[1]
    )
    mine.start()
    dz, dx, dc = Sends(s_dz, r_dz), Sends(s_dx, r_dx), Sends(s_dc, r_dc)
    az, ax, ac = Sends(s_az, r_az), Sends(s_ax, r_ax), Sends(s_ac, r_ac)
    own.wait()
    first.arrived()
    placed = pltpu.make_async_copy(
        panel.at[:, 0], corner.at[:, zh, x, :, zl, core], local.at[2]
    )
    placed.start()
    for device in zs:
        dz.add(panel.at[:, 0], corner.at[:, zh, x, :, zl, core], device)
    dz.start()
    rest.start()
    placed.wait()
    mine.wait()
    dz.arrived()
    for device in xs:
        for a in range(2):
            for b in range(2):
                piece = corner.at[:, a, x, :, b, core]
                dx.add(piece, piece, device)
    dx.start()
    for device in zs:
        az.add(front.at[0, :, :, LANE:], across.at[zh, x, :, zl, core], device)
    dx.arrived()
    for a in range(2):
        for b in range(4):
            for c in range(2):
                piece = corner.at[:, a, b, :, c, core]
                dc.add(piece, piece, other)
    dc.start()
    az.start()
    for device in xs:
        for a in range(2):
            for b in range(2):
                piece = across.at[a, x, :, b, core]
                ax.add(piece, piece, device)
    for a in range(2):
        for b in range(4):
            for c in range(2):
                piece = across.at[a, b, :, c, core]
                ac.add(piece, piece, other)
    dc.arrived()
    for i in range(4):
        matrix[:, i * LANE : (i + 1) * LANE] = corner[i].reshape(WIDTH, LANE)

    def hook(k):
        @pl.when(k == 0)
        def _():
            az.arrived()
            ax.start()

        @pl.when(k == 2)
        def _():
            ax.arrived()
            ac.start()

    inverse_factor(matrix, block, strip, hook)
    rest.arrived()
    for i in range(4):
        wide[:, i * LANE : (i + 1) * LANE] = panel[i].reshape(cycles * 2 * SUB, LANE)
    whole[...] = mm_t(wide[...], matrix[...])
    factor[...] = whole[:, pl.ds(pl.multiple_of(col * LANE, LANE), LANE)]
    wide[...] = mm(whole[...], matrix[...])
    ac.arrived()
    border = cycles - 1
    width = border * LANE
    for begin in range(0, width, 2 * LANE):
        size = min(2 * LANE, width - begin)
        product = mm(
            wide[2 * SUB :, :], across[:, :, :, :, :, :, begin : begin + size].reshape(WIDTH, size)
        ).reshape(border, 2, SUB, size)
        for h in range(2):
            update[h, :, :, begin : begin + size] = (
                front[1:, h, :, LANE + begin : LANE + begin + size] - product[:, h]
            )
    for stage in (first, rest, dz, dx, dc, az, ax, ac):
        stage.left()


def parent_kernel(
    border_map, update, front, factor, tail,
    taken, total, panel, corner, across, matrix, block, strip, wide, whole, local,
    s_p, r_p, s_y, r_y, s_rest, r_rest, s_dz, r_dz, s_dx, r_dx, s_dc, r_dc, s_az, r_az, s_ax, r_ax, s_ac, r_ac,
):
    cube, row, col = place()
    core, zl, child = cube % 2, cube // 2, cube // 4
    x, zh = row % 4, row // 4
    cycles = front.shape[0]
    border = cycles - 1
    partner = ((cube + 4) % 8, row, col)
    ys = [(cube, row, (col + d) % 4) for d in (1, 2, 3)]
    zs = [((zl + d % 4) % 4 * 2 + core, (zh + d // 4) % 2 * 4 + x, col) for d in range(1, 8)]
    xs = [(cube, zh * 4 + (x + d) % 4, col) for d in (1, 2, 3)]
    other = (cube + 1 - 2 * core, row, col)
    greet(ys + zs + xs + [other])

    sibling = Sends(s_p, r_p)
    sibling.add(update.at[1 - child, 0], taken.at[0], partner)
    sibling.add(update.at[1 - child, 1:, :, 0:LANE], taken.at[1:, :, 0:LANE], partner)
    sibling.add(update.at[1 - child, 1:, :, LANE:], taken.at[1:, :, LANE:], partner)
    sibling.start()

    skipped = []
    for index in (child, 1 - child):
        count = cycles * (cycles - 1) // 2
        for i in range(border):
            count = count - border_map[index, i]
        skipped.append(count)

    def shifted(pick, hole, p):
        before = pick(p) if p < border else None
        after = pick(p - 1) if p else None
        if before is None:
            return jnp.where(hole < p, after, 0.0)
        if after is None:
            return jnp.where(hole > p, before, 0.0)
        return jnp.where(hole > p, before, jnp.where(hole < p, after, 0.0))

    sources = (lambda i, j: update[child, i, :, j * LANE : (j + 1) * LANE],
               lambda i, j: taken[i, :, j * LANE : (j + 1) * LANE])

    def assemble(p, q):
        value = front[p, :, q * LANE : (q + 1) * LANE]
        for source, hole in zip(sources, skipped):
            value = value + shifted(
                lambda i: shifted(lambda j: source(i, j), hole, q), hole, p
            )
        total[p, :, q * LANE : (q + 1) * LANE] = value

    sibling.copies[0].wait_recv()
    assemble(0, 0)
    first, rest = Sends(s_y, r_y), Sends(s_rest, r_rest)
    for device in ys:
        first.add(total.at[0, :, 0:LANE], panel.at[col, 0], device)
    for device in ys:
        rest.add(total.at[1:, :, 0:LANE], panel.at[col, 1:], device)
    first.start()
    for q in range(1, cycles):
        assemble(0, q)
    panel[pl.ds(col, 1), 0] = total[0:1, :, 0:LANE]
    dz, dx, dc = Sends(s_dz, r_dz), Sends(s_dx, r_dx), Sends(s_dc, r_dc)
    az, ax, ac = Sends(s_az, r_az), Sends(s_ax, r_ax), Sends(s_ac, r_ac)
    mine = pltpu.make_async_copy(total.at[0, :, LANE:], across.at[zh, x, zl, core], local.at[1])
    mine.start()
    first.arrived()
    placed = pltpu.make_async_copy(panel.at[:, 0], corner.at[:, zh, x, zl, core], local.at[2])
    placed.start()
    for device in zs:
        dz.add(panel.at[:, 0], corner.at[:, zh, x, zl, core], device)
    dz.start()
    sibling.copies[1].wait_recv()
    for p in range(1, cycles):
        assemble(p, 0)
    placed.wait()
    mine.wait()
    dz.arrived()
    for device in xs:
        for a in range(2):
            for b in range(4):
                piece = corner.at[:, a, x, b, core]
                dx.add(piece, piece, device)
    dx.start()
    rest.start()
    panel[pl.ds(col, 1), 1:] = total[1:, :, 0:LANE][None]
    for device in zs:
        az.add(total.at[0, :, LANE:], across.at[zh, x, zl, core], device)
    dx.arrived()
    for a in range(2):
        for b in range(4):
            for c in range(4):
                piece = corner.at[:, a, b, c, core]
                dc.add(piece, piece, other)
    dc.start()
    az.start()
    for device in xs:
        for a in range(2):
            for b in range(4):
                piece = across.at[a, x, b, core]
                ax.add(piece, piece, device)
    for a in range(2):
        for b in range(4):
            for c in range(4):
                piece = across.at[a, b, c, core]
                ac.add(piece, piece, other)
    dc.arrived()
    for i in range(4):
        matrix[:, i * LANE : (i + 1) * LANE] = corner[i].reshape(WIDTH, LANE)

    def hook(k):
        @pl.when(k == 0)
        def _():
            az.arrived()
            ax.start()

        @pl.when(k == 2)
        def _():
            ax.arrived()
            ac.start()

    inverse_factor(matrix, block, strip, hook)
    sibling.copies[2].wait_recv()
    for p in range(1, cycles):
        for q in range(1, cycles):
            assemble(p, q)
    rest.arrived()
    for i in range(4):
        wide[:, i * LANE : (i + 1) * LANE] = panel[i].reshape(cycles * SUB, LANE)
    whole[...] = mm_t(wide[...], matrix[...])
    factor[...] = whole[:, pl.ds(pl.multiple_of(col * LANE, LANE), LANE)]
    wide[...] = mm(whole[...], matrix[...])
    ac.arrived()
    width = border * LANE
    for begin in range(0, width, 2 * LANE):
        size = min(2 * LANE, width - begin)
        product = mm(
            wide[SUB:, :], across[:, :, :, :, :, begin : begin + size].reshape(WIDTH, size)
        ).reshape(border, SUB, size)
        tail[:, :, begin : begin + size] = (
            total[1:, :, LANE + begin : LANE + begin + size] - product
        )
    for stage in (sibling, first, rest, dz, dx, dc, az, ax, ac):
        stage.left()


def pairs(counts):
    return [pltpu.SemaphoreType.DMA((n,)) for n in counts for _ in range(2)]


def shards(child_front, parent_front, border_map):
    cycles = child_front.shape[1]
    border = cycles - 1
    vmem = pl.BlockSpec(memory_space=pltpu.VMEM)
    smem = pl.BlockSpec(memory_space=pltpu.SMEM)
    front = child_front.reshape(cycles, CHILDREN, SUB, cycles * LANE)
    work = [
        pltpu.VMEM((WIDTH, WIDTH), F32),
        pltpu.VMEM((LANE, LANE), F32),
        pltpu.VMEM((LANE, WIDTH), F32),
    ]
    child_factor, update = pl.pallas_call(
        child_kernel,
        out_shape=(
            jax.ShapeDtypeStruct((cycles * CHILDREN * SUB, LANE), F32),
            jax.ShapeDtypeStruct((CHILDREN, border, SUB, border * LANE), F32),
        ),
        in_specs=[vmem],
        out_specs=(vmem, vmem),
        scratch_shapes=[
            pltpu.VMEM((4, cycles, CHILDREN, SUB, LANE), F32),
            pltpu.VMEM((4, 2, 4, CHILDREN, 2, 2, SUB, LANE), F32),
            pltpu.VMEM((2, 4, CHILDREN, 2, 2, SUB, border * LANE), F32),
            *work,
            pltpu.VMEM((cycles * CHILDREN * SUB, WIDTH), F32),
            pltpu.VMEM((cycles * CHILDREN * SUB, WIDTH), F32),
            pltpu.SemaphoreType.DMA((3,)),
            *pairs((3, 3, 3, 12, 16, 3, 12, 16)),
        ],
        compiler_params=pltpu.CompilerParams(collective_id=0, has_side_effects=True),
        name="child_panel",
    )(front)
    parent_cycles = parent_front.shape[0]
    tail_cycles = parent_cycles - 1
    parent_factor, tail = pl.pallas_call(
        parent_kernel,
        out_shape=(
            jax.ShapeDtypeStruct((parent_cycles * SUB, LANE), F32),
            jax.ShapeDtypeStruct((tail_cycles, SUB, tail_cycles * LANE), F32),
        ),
        in_specs=[smem, vmem, vmem],
        out_specs=(vmem, vmem),
        scratch_shapes=[
            pltpu.VMEM((border, SUB, border * LANE), F32),
            pltpu.VMEM((parent_cycles, SUB, parent_cycles * LANE), F32),
            pltpu.VMEM((4, parent_cycles, SUB, LANE), F32),
            pltpu.VMEM((4, 2, 4, 4, 2, SUB, LANE), F32),
            pltpu.VMEM((2, 4, 4, 2, SUB, tail_cycles * LANE), F32),
            *work,
            pltpu.VMEM((parent_cycles * SUB, WIDTH), F32),
            pltpu.VMEM((parent_cycles * SUB, WIDTH), F32),
            pltpu.SemaphoreType.DMA((3,)),
            *pairs((3, 3, 3, 7, 24, 32, 7, 24, 32)),
        ],
        compiler_params=pltpu.CompilerParams(collective_id=1, has_side_effects=True),
        name="parent_panel",
    )(border_map, update, parent_front.reshape(parent_cycles, SUB, parent_cycles * LANE))
    return (
        child_factor.reshape(1, cycles, 1, CHILDREN, SUB, 1, 1, LANE),
        parent_factor.reshape(parent_cycles, 1, 1, SUB, 1, 1, LANE),
        tail.reshape(tail_cycles, 1, 1, SUB, tail_cycles, 1, LANE),
    )


def solution(mesh):
    return jax.shard_map(
        shards,
        mesh=mesh,
        in_specs=(
            P("cube", None, "row", None, None, None, "col", None),
            P(None, "row", "cube", None, None, "col", None),
            P(),
        ),
        out_specs=(
            P("cube", None, "row", None, None, None, "col", None),
            P(None, "row", "cube", None, None, "col", None),
            P(None, "row", "cube", None, None, "col", None),
        ),
        check_vma=False,
    )
```

```python
import functools

import jax
import jax.numpy as jnp
from jax import lax
from jax.experimental import pallas as pl
from jax.experimental.pallas import tpu as pltpu
from jax.sharding import PartitionSpec as P

CHILDREN = 2
SUB = 8
LANE = 128
WIDTH = 512
STEP = 8
HIGHEST = lax.Precision.HIGHEST
MESH = pl.DeviceIdType.MESH
F32 = jnp.float32


def mm(a, b):
    return jnp.dot(a, b, precision=HIGHEST, preferred_element_type=F32)


def mm_t(a, b):
    return lax.dot_general(
        a, b, (((1,), (1,)), ((), ())), precision=HIGHEST, preferred_element_type=F32
    )


def diagonal_inverse(tiles, out_ref, midway):
    rows = list(tiles)
    lane = lax.broadcasted_iota(jnp.int32, (SUB, LANE), 1)
    n = LANE // SUB
    for t in range(n):
        j = t * SUB
        if t == n // 2:
            midway()
        column = [
            {i: jnp.broadcast_to(rows[i][:, j + a : j + a + 1], (SUB, LANE)) for i in range(t, n)}
            for a in range(STEP)
        ]
        inside = (lane >= j) & (lane < j + STEP)
        right = []
        for a in range(STEP):
            row = jnp.broadcast_to(rows[t][a : a + 1, :], (SUB, LANE))
            right.append(jnp.where(lane == j + a, 1.0, jnp.where(inside, 0.0, row)))
        pivot = {
            (a, b): jnp.broadcast_to(column[b][t][a : a + 1, :], (SUB, LANE))
            for a in range(STEP)
            for b in range(a, STEP)
        }
        scaled = []
        for a in range(STEP):
            inverse = 1.0 / pivot[a, a]
            scaled.append(right[a] * inverse)
            row = jnp.where(lane <= j + a, right[a] * lax.rsqrt(pivot[a, a]), 0.0)
            out_ref[j + a : j + a + 1, :] = row[:1, :]
            for b in range(a + 1, STEP):
                ratio = pivot[a, b] * inverse
                right[b] = right[b] - pivot[a, b] * scaled[a]
                for d in range(b, STEP):
                    pivot[b, d] = pivot[b, d] - ratio * pivot[a, d]
                for i in range(t + 1, n):
                    column[b][i] = column[b][i] - column[a][i] * ratio
        for i in range(t + 1, n):
            rest = jnp.where(inside, 0.0, rows[i])
            for a in range(STEP):
                rest = rest - column[a][i] * scaled[a]
            rows[i] = rest


def inverse_factor(matrix, block, strip, midway, after):
    blocks = WIDTH // LANE

    def body(k, carry):
        here = pl.ds(pl.multiple_of(k * LANE, LANE), LANE)
        tiles = [
            matrix[pl.ds(pl.multiple_of(k * LANE + SUB * i, SUB), SUB), here]
            for i in range(LANE // SUB)
        ]
        diagonal_inverse(tiles, block, lambda: midway(k))
        after(k)
        strip[...] = mm(block[...], matrix[here, :])
        strip[:, here] = block[...]
        for i in range(1, blocks):
            below = slice(i * LANE, (i + 1) * LANE)

            @pl.when(k < i)
            def _():
                left = mm_t(matrix[below, here], block[...])
                matrix[below, here] = jnp.zeros((LANE, LANE), F32)
                matrix[below, :] = matrix[below, :] - mm(left, strip[...])

        for i in range(blocks):
            columns = slice(i * LANE, (i + 1) * LANE)
            matrix[here, columns] = jnp.where(k >= i, strip[:, columns], 0.0)
        return carry

    lax.fori_loop(0, blocks, body, 0)


class Sends:
    def __init__(self, send, recv):
        self.send, self.recv, self.copies = send, recv, []

    def add(self, src, dst, device):
        index = len(self.copies)
        copy = pltpu.make_async_remote_copy(
            src_ref=src,
            dst_ref=dst,
            send_sem=self.send.at[index],
            recv_sem=self.recv.at[index],
            device_id=device,
            device_id_type=MESH,
        )
        self.copies.append(copy)

    def start(self):
        for copy in self.copies:
            copy.start()

    def arrived(self):
        for copy in self.copies:
            copy.wait_recv()

    def left(self):
        for copy in self.copies:
            copy.wait_send()


def greet(peers):
    barrier = pltpu.get_barrier_semaphore()
    for device in peers:
        pl.semaphore_signal(barrier, inc=1, device_id=device, device_id_type=MESH)
    pl.semaphore_wait(barrier, len(peers))


def fill(matrix, corner, first, last):
    for i in range(first, last):
        matrix[:, i * LANE : (i + 1) * LANE] = corner[i].reshape(WIDTH, LANE)


class Panel:
    def __init__(self, corner, across, near, line, xs, other, own, band, core, sems):
        self.corner, self.across, self.core = corner, across, core
        self.near, self.line, self.xs, self.other = near, line, xs, other
        self.own, self.band = own, band
        (self.dz, self.dx0, self.dx1, self.dc0, self.dc1,
         self.az, self.ax0, self.ax1, self.ac0, self.ac1) = (Sends(*pair) for pair in sems)
        width = across.shape[-1]
        self.cut = width // 2 // LANE * LANE

    def stages(self):
        return (self.dz, self.dx0, self.dx1, self.dc0, self.dc1,
                self.az, self.ax0, self.ax1, self.ac0, self.ac1)

    def corner_out(self, tile):
        for device in self.near:
            self.dz.add(tile, self.own(self.corner), device)
        self.dz.start()

    def across_out(self, strip):
        for device in self.line:
            self.az.add(strip, self.band(self.across), device)
        self.az.start()

    def corner_on(self, along_x, along_core):
        self.dz.arrived()
        for device in self.xs:
            piece = along_x(self.corner, slice(0, 1))
            self.dx0.add(piece, piece, device)
        for device in self.xs:
            piece = along_x(self.corner, slice(1, 4))
            self.dx1.add(piece, piece, device)
        self.dx0.start()
        self.dx1.start()
        self.dx0.arrived()
        piece = along_core(self.corner, slice(0, 1))
        self.dc0.add(piece, piece, self.other)
        self.dc0.start()
        piece = along_core(self.corner, slice(1, 4))
        self.dc1.add(piece, piece, self.other)
        self.along = (along_x, along_core)

    def prepare_across(self, along_x, along_core):
        parts = (slice(0, self.cut), slice(self.cut, None))
        for part, ax, ac in zip(parts, (self.ax0, self.ax1), (self.ac0, self.ac1)):
            for device in self.xs:
                piece = along_x(self.across, part)
                ax.add(piece, piece, device)
            piece = along_core(self.across, part)
            ac.add(piece, piece, self.other)

    def factor(self, matrix, block, strip, also):
        self.dc0.arrived()
        fill(matrix, self.corner, 0, 1)

        def midway(k):
            @pl.when(k == 0)
            def _():
                self.dx1.arrived()
                self.dc1.start()
                self.az.arrived()
                self.ax0.start()
                self.ax1.start()
                also()

        def after(k):
            @pl.when(k == 0)
            def _():
                self.dc1.arrived()
                fill(matrix, self.corner, 1, 4)

            @pl.when(k == 1)
            def _():
                self.ax0.arrived()
                self.ac0.start()

            @pl.when(k == 2)
            def _():
                self.ax1.arrived()
                self.ac1.start()

        inverse_factor(matrix, block, strip, midway, after)


def kernel(
    border_map, child_in, parent_in, child_factor, parent_factor, tail,
    front, c_panel, c_corner, c_across, update,
    taken, total, p_panel, p_corner, p_across,
    matrix, block, strip, wide, whole, local, *sems,
):
    cube, row, col = lax.axis_index("cube"), lax.axis_index("row"), lax.axis_index("col")
    core, zl, child = cube % 2, cube // 2, cube // 4
    half = zl % 2
    x, zh = row % 4, row // 4
    cycles = front.shape[0]
    border = cycles - 1
    width = border * LANE

    def at(dz, dh, dy):
        return ((zl + dz) % 4 * 2 + core, (zh + dh) % 2 * 4 + x, (col + dy) % 4)

    def at_half(dz, dh, dy):
        return (child * 4 + (half + dz) % 2 * 2 + core, (zh + dh) % 2 * 4 + x, (col + dy) % 4)

    c_near = [at_half(a, b, d) for a in range(2) for b in range(2) for d in range(4) if a + b + d]
    p_near = [at(a, b, d) for a in range(4) for b in range(2) for d in range(4) if a + b + d]
    c_line = [at_half(a, b, 0) for a in range(2) for b in range(2) if a + b]
    p_line = [at(a, b, 0) for a in range(4) for b in range(2) if a + b]
    ys = [at(0, 0, d) for d in (1, 2, 3)]
    xs = [(cube, zh * 4 + (x + d) % 4, col) for d in (1, 2, 3)]
    other = (cube + 1 - 2 * core, row, col)
    partner = ((cube + 4) % 8, row, col)
    pairs_of = [(sems[2 * i], sems[2 * i + 1]) for i in range(len(sems) // 2)]
    greet(p_near + xs + [other])

    def lay(t):
        for h in range(CHILDREN):
            for s in range(cycles):
                start = ((t * CHILDREN + h) * SUB) * cycles + s
                front[t, h, :, s * LANE : (s + 1) * LANE] = child_in[
                    pl.ds(start, SUB, stride=cycles), :
                ]

    child_side = Panel(
        c_corner, c_across, c_near, c_line, xs, other,
        lambda ref: ref.at[col, zh, x, :, half, core],
        lambda ref: ref.at[zh, x, :, half, core],
        core, pairs_of[0:10],
    )
    lay(0)
    child_side.corner_out(front.at[0, :, :, 0:LANE])
    child_side.across_out(front.at[0, :, :, LANE:])
    own = front[0]
    c_corner[pl.ds(col, 1), pl.ds(zh, 1), pl.ds(x, 1), :, pl.ds(half, 1), pl.ds(core, 1)] = own[
        :, :, 0:LANE
    ].reshape(1, 1, 1, CHILDREN, 1, 1, SUB, LANE)
    c_across[pl.ds(zh, 1), pl.ds(x, 1), :, pl.ds(half, 1), pl.ds(core, 1)] = own[
        :, :, LANE:
    ].reshape(1, 1, CHILDREN, 1, 1, SUB, width)
    for t in range(1, cycles):
        lay(t)
    c_rest = Sends(*pairs_of[20])
    for device in ys:
        c_rest.add(front.at[:, :, :, 0:LANE], c_panel.at[col], device)
    c_rest.start()
    c_panel[pl.ds(col, 1)] = front[:, :, :, 0:LANE][None]
    child_side.corner_on(
        lambda ref, part: ref.at[part, :, x, :, :, core],
        lambda ref, part: ref.at[part, :, :, :, :, core],
    )
    child_side.prepare_across(
        lambda ref, part: ref.at[:, x, :, :, core, :, part],
        lambda ref, part: ref.at[:, :, :, :, core, :, part],
    )
    child_side.factor(matrix, block, strip, lambda: None)

    c_rest.arrived()
    for i in range(4):
        wide[:, i * LANE : (i + 1) * LANE] = c_panel[i].reshape(cycles * CHILDREN * SUB, LANE)
    whole[...] = mm_t(wide[...], matrix[...])
    wide[...] = mm(whole[...], matrix[...])
    child_side.ac0.arrived()

    def child_update(first, last, begin, end):
        for left in range(begin, end, 2 * LANE):
            size = min(2 * LANE, end - left)
            product = mm(
                wide[(first + 1) * CHILDREN * SUB : (last + 1) * CHILDREN * SUB, :],
                c_across[:, :, :, :, :, :, left : left + size].reshape(WIDTH, size),
            ).reshape(last - first, CHILDREN, SUB, size)
            for h in range(CHILDREN):
                update[h, first:last, :, left : left + size] = (
                    front[first + 1 : last + 1, h, :, LANE + left : LANE + left + size]
                    - product[:, h]
                )

    sibling = Sends(*pairs_of[21])
    for rows, columns in (
        (slice(0, 1), slice(0, LANE)),
        (slice(0, 1), slice(LANE, None)),
        (slice(1, None), slice(0, LANE)),
        (slice(1, None), slice(LANE, None)),
    ):
        sibling.add(
            update.at[1 - child, rows, :, columns], taken.at[rows, :, columns], partner
        )
    child_update(0, 1, 0, LANE)
    sibling.copies[0].start()
    child_side.ac1.arrived()
    child_update(0, 1, LANE, width)
    sibling.copies[1].start()
    child_update(1, border, 0, LANE)
    sibling.copies[2].start()

    holes = []
    for index in (child, 1 - child):
        hole = cycles * (cycles - 1) // 2
        for i in range(border):
            hole = hole - border_map[index, i]
        holes.append(hole)

    def shifted(pick, hole, p):
        if p == 0:
            return jnp.where(hole > 0, pick(0), 0.0)
        if p == border:
            return jnp.where(hole < p, pick(p - 1), 0.0)
        return jnp.where(hole > p, pick(p), jnp.where(hole < p, pick(p - 1), 0.0))

    sources = (
        lambda i, j: update[child, i, :, j * LANE : (j + 1) * LANE],
        lambda i, j: taken[i, :, j * LANE : (j + 1) * LANE],
    )

    def assemble(p, q):
        value = parent_in[pl.ds(p * SUB * cycles + q, SUB, stride=cycles), :]
        for source, hole in zip(sources, holes):
            value = value + shifted(lambda i: shifted(lambda j: source(i, j), hole, q), hole, p)
        total[p, :, q * LANE : (q + 1) * LANE] = value

    parent_side = Panel(
        p_corner, p_across, p_near, p_line, xs, other,
        lambda ref: ref.at[col, zh, x, zl, core],
        lambda ref: ref.at[zh, x, zl, core],
        core, pairs_of[10:20],
    )
    sibling.copies[0].wait_recv()
    assemble(0, 0)
    parent_side.corner_out(total.at[0, :, 0:LANE])
    sibling.copies[1].wait_recv()
    for q in range(1, cycles):
        assemble(0, q)
    parent_side.across_out(total.at[0, :, LANE:])
    own = total[0]
    p_corner[pl.ds(col, 1), pl.ds(zh, 1), pl.ds(x, 1), pl.ds(zl, 1), pl.ds(core, 1)] = own[
        :, 0:LANE
    ].reshape(1, 1, 1, 1, 1, SUB, LANE)
    p_across[pl.ds(zh, 1), pl.ds(x, 1), pl.ds(zl, 1), pl.ds(core, 1)] = own[:, LANE:].reshape(
        1, 1, 1, 1, SUB, width
    )
    sibling.copies[2].wait_recv()
    for p in range(1, cycles):
        assemble(p, 0)
    p_rest = Sends(*pairs_of[22])
    for device in ys:
        p_rest.add(total.at[:, :, 0:LANE], p_panel.at[col], device)
    p_rest.start()
    p_panel[pl.ds(col, 1)] = total[:, :, 0:LANE][None]
    child_update(1, border, LANE, width)
    child_factor[...] = whole[:, pl.ds(pl.multiple_of(col * LANE, LANE), LANE)]
    parent_side.corner_on(
        lambda ref, part: ref.at[part, :, x, :, core],
        lambda ref, part: ref.at[part, :, :, :, core],
    )
    parent_side.prepare_across(
        lambda ref, part: ref.at[:, x, :, core, :, part],
        lambda ref, part: ref.at[:, :, :, core, :, part],
    )
    parent_side.factor(matrix, block, strip, lambda: sibling.copies[3].start())

    p_rest.arrived()
    rows = cycles * SUB
    for i in range(4):
        wide[:rows, i * LANE : (i + 1) * LANE] = p_panel[i].reshape(rows, LANE)
    whole[:rows, :] = mm_t(wide[:rows, :], matrix[...])
    wide[:rows, :] = mm(whole[:rows, :], matrix[...])
    parent_factor[...] = whole[:rows, pl.ds(pl.multiple_of(col * LANE, LANE), LANE)]
    sibling.copies[3].wait_recv()
    for p in range(1, cycles):
        for q in range(1, cycles):
            assemble(p, q)
    parent_side.ac0.arrived()
    parent_side.ac1.arrived()
    for left in range(0, width, 2 * LANE):
        size = min(2 * LANE, width - left)
        product = mm(
            wide[SUB:rows, :], p_across[:, :, :, :, :, left : left + size].reshape(WIDTH, size)
        ).reshape(border, SUB, size)
        value = total[1:, :, LANE + left : LANE + left + size] - product
        for p in range(border):
            for q in range(size // LANE):
                tail[pl.ds(p * SUB * border + left // LANE + q, SUB, stride=border), :] = value[
                    p, :, q * LANE : (q + 1) * LANE
                ]
    for stage in (*child_side.stages(), *parent_side.stages(), c_rest, sibling, p_rest):
        stage.left()


def shards(child_front, parent_front, border_map):
    cycles = child_front.shape[1]
    border = cycles - 1
    vmem = pl.BlockSpec(memory_space=pltpu.VMEM)
    smem = pl.BlockSpec(memory_space=pltpu.SMEM)
    counts = [15, 3, 3, 1, 1, 3, 3, 3, 1, 1, 31, 3, 3, 1, 1, 7, 3, 3, 1, 1, 3, 4, 3]
    child_factor, parent_factor, tail = pl.pallas_call(
        kernel,
        out_shape=(
            jax.ShapeDtypeStruct((cycles * CHILDREN * SUB, LANE), F32),
            jax.ShapeDtypeStruct((cycles * SUB, LANE), F32),
            jax.ShapeDtypeStruct((border * SUB * border, LANE), F32),
        ),
        in_specs=[smem, vmem, vmem],
        out_specs=(vmem, vmem, vmem),
        scratch_shapes=[
            pltpu.VMEM((cycles, CHILDREN, SUB, cycles * LANE), F32),
            pltpu.VMEM((4, cycles, CHILDREN, SUB, LANE), F32),
            pltpu.VMEM((4, 2, 4, CHILDREN, 2, 2, SUB, LANE), F32),
            pltpu.VMEM((2, 4, CHILDREN, 2, 2, SUB, border * LANE), F32),
            pltpu.VMEM((CHILDREN, border, SUB, border * LANE), F32),
            pltpu.VMEM((border, SUB, border * LANE), F32),
            pltpu.VMEM((cycles, SUB, cycles * LANE), F32),
            pltpu.VMEM((4, cycles, SUB, LANE), F32),
            pltpu.VMEM((4, 2, 4, 4, 2, SUB, LANE), F32),
            pltpu.VMEM((2, 4, 4, 2, SUB, border * LANE), F32),
            pltpu.VMEM((WIDTH, WIDTH), F32),
            pltpu.VMEM((LANE, LANE), F32),
            pltpu.VMEM((LANE, WIDTH), F32),
            pltpu.VMEM((cycles * CHILDREN * SUB, WIDTH), F32),
            pltpu.VMEM((cycles * CHILDREN * SUB, WIDTH), F32),
            pltpu.SemaphoreType.DMA((1,)),
            *(pltpu.SemaphoreType.DMA((n,)) for n in counts for _ in range(2)),
        ],
        compiler_params=pltpu.CompilerParams(collective_id=0, has_side_effects=True),
        name="fronts",
    )(
        border_map,
        child_front.reshape(cycles * CHILDREN * SUB * cycles, LANE),
        parent_front.reshape(cycles * SUB * cycles, LANE),
    )
    return (
        child_factor.reshape(1, cycles, 1, CHILDREN, SUB, 1, 1, LANE),
        parent_factor.reshape(cycles, 1, 1, SUB, 1, 1, LANE),
        tail.reshape(border, 1, 1, SUB, border, 1, LANE),
    )


def solution(mesh):
    return jax.shard_map(
        shards,
        mesh=mesh,
        in_specs=(
            P("cube", None, "row", None, None, None, "col", None),
            P(None, "row", "cube", None, None, "col", None),
            P(),
        ),
        out_specs=(
            P("cube", None, "row", None, None, None, "col", None),
            P(None, "row", "cube", None, None, "col", None),
            P(None, "row", "cube", None, None, "col", None),
        ),
        check_vma=False,
    )
```

```python
import functools

import jax
import jax.numpy as jnp
from jax import lax
from jax.experimental import pallas as pl
from jax.experimental.pallas import tpu as pltpu
from jax.sharding import PartitionSpec as P

CHILDREN = 2
SUB = 8
LANE = 128
WIDTH = 512
STEP = 8
HIGHEST = lax.Precision.HIGHEST
MESH = pl.DeviceIdType.MESH
F32 = jnp.float32


def mm(a, b):
    return jnp.dot(a, b, precision=HIGHEST, preferred_element_type=F32)


def mm_t(a, b):
    return lax.dot_general(
        a, b, (((1,), (1,)), ((), ())), precision=HIGHEST, preferred_element_type=F32
    )


def diagonal_inverse(tiles, out_ref, midway):
    rows = list(tiles)
    lane = lax.broadcasted_iota(jnp.int32, (SUB, LANE), 1)
    n = LANE // SUB

    def across_lanes(tile, index):
        picks = jnp.full((SUB, LANE), index, jnp.int32)
        return jnp.take_along_axis(tile, picks, axis=1, mode="promise_in_bounds")

    def across_rows(tile, index):
        return jnp.broadcast_to(tile[index : index + 1, :], (SUB, LANE))

    for t in range(n):
        j = t * SUB
        if t == n // 2:
            midway()
        inside = (lane >= j) & (lane < j + STEP)
        near = range(t + 1, min(n, t + 2))
        column = [across_lanes(rows[t], j + a) for a in range(STEP)]
        below = {i: [across_lanes(rows[i], j + a) for a in range(STEP)] for i in near}
        rest = {i: jnp.where(inside, 0.0, rows[i]) for i in range(t + 1, n)}
        right = [
            jnp.where(lane == j + a, 1.0, jnp.where(inside, 0.0, across_rows(rows[t], a)))
            for a in range(STEP)
        ]
        pivot = {
            (a, b): across_rows(column[b], a) for a in range(STEP) for b in range(a, STEP)
        }
        scaled, ratio = [], {}
        for a in range(STEP):
            inverse = 1.0 / pivot[a, a]
            scaled.append(right[a] * inverse)
            row = jnp.where(lane <= j + a, right[a] * lax.rsqrt(pivot[a, a]), 0.0)
            out_ref[j + a : j + a + 1, :] = row[:1, :]
            for b in range(a + 1, STEP):
                ratio[a, b] = pivot[a, b] * inverse
                for d in range(b, STEP):
                    pivot[b, d] = pivot[b, d] - ratio[a, b] * pivot[a, d]
                right[b] = right[b] - pivot[a, b] * scaled[a]
                for i in near:
                    below[i][b] = below[i][b] - below[i][a] * ratio[a, b]
            for i in near:
                rest[i] = rest[i] - below[i][a] * scaled[a]
        if t + 2 < n:
            for b in range(STEP - 1, 0, -1):
                for a in range(b):
                    scaled[a] = scaled[a] - ratio[a, b] * scaled[b]
        for i in range(t + 2, n):
            for a in range(STEP):
                rest[i] = rest[i] - across_lanes(rows[i], j + a) * scaled[a]
        for i in range(t + 1, n):
            rows[i] = rest[i]


def inverse_factor(matrix, block, strip, midway, after):
    blocks = WIDTH // LANE

    def body(k, carry):
        here = pl.ds(pl.multiple_of(k * LANE, LANE), LANE)
        tiles = [
            matrix[pl.ds(pl.multiple_of(k * LANE + SUB * i, SUB), SUB), here]
            for i in range(LANE // SUB)
        ]
        diagonal_inverse(tiles, block, lambda: midway(k))
        after(k)
        strip[...] = mm(block[...], matrix[here, :])
        strip[:, here] = block[...]
        for i in range(1, blocks):
            below = slice(i * LANE, (i + 1) * LANE)

            @pl.when(k < i)
            def _():
                left = mm_t(matrix[below, here], block[...])
                matrix[below, here] = jnp.zeros((LANE, LANE), F32)
                matrix[below, :] = matrix[below, :] - mm(left, strip[...])

        for i in range(blocks):
            columns = slice(i * LANE, (i + 1) * LANE)
            matrix[here, columns] = jnp.where(k >= i, strip[:, columns], 0.0)
        return carry

    lax.fori_loop(0, blocks, body, 0)


class Sends:
    def __init__(self, send, recv):
        self.send, self.recv, self.copies = send, recv, []

    def add(self, src, dst, device):
        index = len(self.copies)
        copy = pltpu.make_async_remote_copy(
            src_ref=src,
            dst_ref=dst,
            send_sem=self.send.at[index],
            recv_sem=self.recv.at[index],
            device_id=device,
            device_id_type=MESH,
        )
        self.copies.append(copy)

    def start(self):
        for copy in self.copies:
            copy.start()

    def arrived(self):
        for copy in self.copies:
            copy.wait_recv()

    def left(self):
        for copy in self.copies:
            copy.wait_send()


def greet(peers):
    barrier = pltpu.get_barrier_semaphore()
    for device in peers:
        pl.semaphore_signal(barrier, inc=1, device_id=device, device_id_type=MESH)
    pl.semaphore_wait(barrier, len(peers))


def fill(matrix, corner, first, last):
    for i in range(first, last):
        matrix[:, i * LANE : (i + 1) * LANE] = corner[i].reshape(WIDTH, LANE)


class Panel:
    def __init__(self, corner, across, near, line, xs, other, own, band, sems):
        self.corner, self.across = corner, across
        self.near, self.line, self.xs, self.other = near, line, xs, other
        self.own, self.band = own, band
        (self.dz, self.dx0, self.dx1, self.dc0, self.dc1, self.az, self.ring, self.on, self.ac) = (
            Sends(*pair) for pair in sems
        )

    def stages(self):
        return (
            self.dz, self.dx0, self.dx1, self.dc0, self.dc1, self.az, self.ring, self.on, self.ac
        )

    def corner_out(self, tile):
        for device in self.near:
            self.dz.add(tile, self.own(self.corner), device)
        self.dz.start()

    def across_out(self, strip):
        for device in self.line:
            self.az.add(strip, self.band(self.across), device)
        self.az.start()

    def corner_on(self, along_x, along_core):
        self.dz.arrived()
        for stage, part in ((self.dx0, slice(0, 1)), (self.dx1, slice(1, 4))):
            piece = along_x(self.corner, part)
            for device in self.xs:
                stage.add(piece, piece, device)
            stage.start()
        for stage, part in ((self.dc0, slice(0, 1)), (self.dc1, slice(1, 4))):
            piece = along_core(self.corner, part)
            stage.add(piece, piece, self.other)
        self.dx0.arrived()
        self.dc0.start()

    def prepare_across(self, x, block):
        cut = self.across.shape[-1] // 2 // LANE * LANE
        half = (slice(0, cut), slice(cut, None))
        right, left = self.xs[0], self.xs[2]
        for device, part in ((right, 0), (left, 1), (right, 1), (left, 0)):
            piece = block(x, half[part])
            self.ring.add(piece, piece, device)
        piece = block((x + 3) % 4, half[0])
        self.on.add(piece, piece, right)
        piece = block((x + 1) % 4, half[1])
        self.on.add(piece, piece, left)
        for d in (0, 1, 3, 2):
            piece = block((x + d) % 4, slice(None))
            self.ac.add(piece, piece, self.other)

    def factor(self, matrix, block, strip, also):
        self.dc0.arrived()
        fill(matrix, self.corner, 0, 1)

        def midway(k):
            @pl.when(k == 0)
            def _():
                self.dx1.arrived()
                self.dc1.start()
                self.az.arrived()
                self.ring.start()
                also()

            @pl.when(k == 3)
            def _():
                self.on.arrived()
                self.ac.copies[3].start()

        def after(k):
            @pl.when(k == 0)
            def _():
                self.dc1.arrived()
                fill(matrix, self.corner, 1, 4)

            @pl.when(k == 1)
            def _():
                for copy in self.ring.copies[:2]:
                    copy.wait_recv()
                self.on.start()

            @pl.when(k == 2)
            def _():
                for copy in self.ring.copies[2:]:
                    copy.wait_recv()
                for copy in self.ac.copies[:3]:
                    copy.start()

        inverse_factor(matrix, block, strip, midway, after)


def kernel(
    border_map, child_hbm, parent_hbm, child_factor, parent_factor, tail,
    child_in, parent_in, front, c_panel, c_corner, c_across, update,
    taken, total, p_panel, p_corner, p_across,
    matrix, block, strip, wide, whole, local, *sems,
):
    cube, row, col = lax.axis_index("cube"), lax.axis_index("row"), lax.axis_index("col")
    core, zl, child = cube % 2, cube // 2, cube // 4
    half = zl % 2
    x, zh = row % 4, row // 4
    cycles = front.shape[0]
    border = cycles - 1
    width = border * LANE

    def at(dz, dh, dy):
        return ((zl + dz) % 4 * 2 + core, (zh + dh) % 2 * 4 + x, (col + dy) % 4)

    def at_half(dz, dh, dy):
        return (child * 4 + (half + dz) % 2 * 2 + core, (zh + dh) % 2 * 4 + x, (col + dy) % 4)

    c_near = [at_half(a, b, d) for a in range(2) for b in range(2) for d in range(4) if a + b + d]
    p_near = [at(a, b, d) for a in range(4) for b in range(2) for d in range(4) if a + b + d]
    c_line = [at_half(a, b, 0) for a in range(2) for b in range(2) if a + b]
    p_line = [at(a, b, 0) for a in range(4) for b in range(2) if a + b]
    ys = [at(0, 0, d) for d in (1, 2, 3)]
    xs = [(cube, zh * 4 + (x + d) % 4, col) for d in (1, 2, 3)]
    other = (cube + 1 - 2 * core, row, col)
    partner = ((cube + 4) % 8, row, col)
    pairs_of = [(sems[2 * i], sems[2 * i + 1]) for i in range(len(sems) // 2)]
    def lay(t):
        for h in range(CHILDREN):
            for s in range(cycles):
                start = ((t * CHILDREN + h) * SUB) * cycles + s
                front[t, h, :, s * LANE : (s + 1) * LANE] = child_in[
                    pl.ds(start, SUB, stride=cycles), :
                ]

    head = CHILDREN * SUB * cycles
    loads = [
        pltpu.make_async_copy(child_hbm.at[:head], child_in.at[:head], local.at[0]),
        pltpu.make_async_copy(child_hbm.at[head:], child_in.at[head:], local.at[1]),
        pltpu.make_async_copy(parent_hbm, parent_in, local.at[2]),
    ]
    for load in loads:
        load.start()
    loads[0].wait()
    lay(0)
    greet(p_near + xs + [other])

    child_side = Panel(
        c_corner, c_across, c_near, c_line, xs, other,
        lambda ref: ref.at[col, zh, x, :, half, core],
        lambda ref: ref.at[zh, x, :, half, core],
        pairs_of[0:9],
    )
    child_side.corner_out(front.at[0, :, :, 0:LANE])
    child_side.across_out(front.at[0, :, :, LANE:])
    own = front[0]
    c_corner[pl.ds(col, 1), pl.ds(zh, 1), pl.ds(x, 1), :, pl.ds(half, 1), pl.ds(core, 1)] = own[
        :, :, 0:LANE
    ].reshape(1, 1, 1, CHILDREN, 1, 1, SUB, LANE)
    c_across[pl.ds(zh, 1), pl.ds(x, 1), :, pl.ds(half, 1), pl.ds(core, 1)] = own[
        :, :, LANE:
    ].reshape(1, 1, CHILDREN, 1, 1, SUB, width)
    loads[1].wait()
    for t in range(1, cycles):
        lay(t)
    loads[2].wait()
    c_rest = Sends(*pairs_of[18])
    for device in ys:
        c_rest.add(front.at[:, :, :, 0:LANE], c_panel.at[col], device)
    c_rest.start()
    c_panel[pl.ds(col, 1)] = front[:, :, :, 0:LANE][None]
    child_side.corner_on(
        lambda ref, part: ref.at[part, :, x, :, :, core],
        lambda ref, part: ref.at[part, :, :, :, :, core],
    )
    child_side.prepare_across(x, lambda at_x, part: c_across.at[:, at_x, :, :, core, :, part])
    child_side.factor(matrix, block, strip, lambda: None)

    c_rest.arrived()
    for i in range(4):
        wide[:, i * LANE : (i + 1) * LANE] = c_panel[i].reshape(cycles * CHILDREN * SUB, LANE)
    whole[...] = mm_t(wide[...], matrix[...])
    wide[...] = mm(whole[...], matrix[...])
    child_side.ac.arrived()

    def child_update(first, last, begin, end):
        for left in range(begin, end, 2 * LANE):
            size = min(2 * LANE, end - left)
            product = mm(
                wide[(first + 1) * CHILDREN * SUB : (last + 1) * CHILDREN * SUB, :],
                c_across[:, :, :, :, :, :, left : left + size].reshape(WIDTH, size),
            ).reshape(last - first, CHILDREN, SUB, size)
            for h in range(CHILDREN):
                update[h, first:last, :, left : left + size] = (
                    front[first + 1 : last + 1, h, :, LANE + left : LANE + left + size]
                    - product[:, h]
                )

    sibling = Sends(*pairs_of[19])
    for rows, columns in (
        (slice(0, 1), slice(0, LANE)),
        (slice(0, 1), slice(LANE, None)),
        (slice(1, None), slice(0, LANE)),
        (slice(1, None), slice(LANE, None)),
    ):
        sibling.add(
            update.at[1 - child, rows, :, columns], taken.at[rows, :, columns], partner
        )
    child_update(0, 1, 0, LANE)
    sibling.copies[0].start()
    child_update(0, 1, LANE, width)
    sibling.copies[1].start()
    child_update(1, border, 0, LANE)
    sibling.copies[2].start()

    holes = []
    for index in (child, 1 - child):
        hole = cycles * (cycles - 1) // 2
        for i in range(border):
            hole = hole - border_map[index, i]
        holes.append(hole)

    def shifted(pick, hole, p):
        if p == 0:
            return jnp.where(hole > 0, pick(0), 0.0)
        if p == border:
            return jnp.where(hole < p, pick(p - 1), 0.0)
        return jnp.where(hole > p, pick(p), jnp.where(hole < p, pick(p - 1), 0.0))

    sources = (
        lambda i, j: update[child, i, :, j * LANE : (j + 1) * LANE],
        lambda i, j: taken[i, :, j * LANE : (j + 1) * LANE],
    )

    def assemble(p, q):
        value = parent_in[pl.ds(p * SUB * cycles + q, SUB, stride=cycles), :]
        for source, hole in zip(sources, holes):
            value = value + shifted(lambda i: shifted(lambda j: source(i, j), hole, q), hole, p)
        total[p, :, q * LANE : (q + 1) * LANE] = value

    parent_side = Panel(
        p_corner, p_across, p_near, p_line, xs, other,
        lambda ref: ref.at[col, zh, x, zl, core],
        lambda ref: ref.at[zh, x, zl, core],
        pairs_of[9:18],
    )
    sibling.copies[0].wait_recv()
    assemble(0, 0)
    parent_side.corner_out(total.at[0, :, 0:LANE])
    sibling.copies[1].wait_recv()
    for q in range(1, cycles):
        assemble(0, q)
    parent_side.across_out(total.at[0, :, LANE:])
    own = total[0]
    p_corner[pl.ds(col, 1), pl.ds(zh, 1), pl.ds(x, 1), pl.ds(zl, 1), pl.ds(core, 1)] = own[
        :, 0:LANE
    ].reshape(1, 1, 1, 1, 1, SUB, LANE)
    p_across[pl.ds(zh, 1), pl.ds(x, 1), pl.ds(zl, 1), pl.ds(core, 1)] = own[:, LANE:].reshape(
        1, 1, 1, 1, SUB, width
    )
    sibling.copies[2].wait_recv()
    for p in range(1, cycles):
        assemble(p, 0)
    p_rest = Sends(*pairs_of[20])
    for device in ys:
        p_rest.add(total.at[:, :, 0:LANE], p_panel.at[col], device)
    p_rest.start()
    p_panel[pl.ds(col, 1)] = total[:, :, 0:LANE][None]
    child_update(1, border, LANE, width)
    child_factor[...] = whole[:, pl.ds(pl.multiple_of(col * LANE, LANE), LANE)]
    parent_side.corner_on(
        lambda ref, part: ref.at[part, :, x, :, core],
        lambda ref, part: ref.at[part, :, :, :, core],
    )
    parent_side.prepare_across(x, lambda at_x, part: p_across.at[:, at_x, :, core, :, part])
    parent_side.factor(matrix, block, strip, lambda: sibling.copies[3].start())

    p_rest.arrived()
    rows = cycles * SUB
    for i in range(4):
        wide[:rows, i * LANE : (i + 1) * LANE] = p_panel[i].reshape(rows, LANE)
    whole[:rows, :] = mm_t(wide[:rows, :], matrix[...])
    wide[:rows, :] = mm(whole[:rows, :], matrix[...])
    parent_factor[...] = whole[:rows, pl.ds(pl.multiple_of(col * LANE, LANE), LANE)]
    sibling.copies[3].wait_recv()
    for p in range(1, cycles):
        for q in range(1, cycles):
            assemble(p, q)
    parent_side.ac.arrived()
    for left in range(0, width, 2 * LANE):
        size = min(2 * LANE, width - left)
        product = mm(
            wide[SUB:rows, :], p_across[:, :, :, :, :, left : left + size].reshape(WIDTH, size)
        ).reshape(border, SUB, size)
        value = total[1:, :, LANE + left : LANE + left + size] - product
        for p in range(border):
            for q in range(size // LANE):
                tail[pl.ds(p * SUB * border + left // LANE + q, SUB, stride=border), :] = value[
                    p, :, q * LANE : (q + 1) * LANE
                ]
    for stage in (*child_side.stages(), *parent_side.stages(), c_rest, sibling, p_rest):
        stage.left()


def hand_on(first, second, third, first_out, second_out, third_out):
    first_out[...] = first[...]
    second_out[...] = second[...]
    third_out[...] = third[...]


def shards(child_front, parent_front, border_map):
    cycles = child_front.shape[1]
    border = cycles - 1
    vmem = pl.BlockSpec(memory_space=pltpu.VMEM)
    smem = pl.BlockSpec(memory_space=pltpu.SMEM)
    kept = pl.BlockSpec(memory_space=pl.ANY)
    counts = [15, 3, 3, 1, 1, 3, 4, 2, 4, 31, 3, 3, 1, 1, 7, 4, 2, 4, 3, 4, 3]
    child_factor, parent_factor, tail = pl.pallas_call(
        kernel,
        out_shape=(
            jax.ShapeDtypeStruct((cycles * CHILDREN * SUB, LANE), F32),
            jax.ShapeDtypeStruct((cycles * SUB, LANE), F32),
            jax.ShapeDtypeStruct((border * SUB * border, LANE), F32),
        ),
        in_specs=[smem, kept, kept],
        out_specs=(vmem, vmem, vmem),
        scratch_shapes=[
            pltpu.VMEM((cycles * CHILDREN * SUB * cycles, LANE), F32),
            pltpu.VMEM((cycles * SUB * cycles, LANE), F32),
            pltpu.VMEM((cycles, CHILDREN, SUB, cycles * LANE), F32),
            pltpu.VMEM((4, cycles, CHILDREN, SUB, LANE), F32),
            pltpu.VMEM((4, 2, 4, CHILDREN, 2, 2, SUB, LANE), F32),
            pltpu.VMEM((2, 4, CHILDREN, 2, 2, SUB, border * LANE), F32),
            pltpu.VMEM((CHILDREN, border, SUB, border * LANE), F32),
            pltpu.VMEM((border, SUB, border * LANE), F32),
            pltpu.VMEM((cycles, SUB, cycles * LANE), F32),
            pltpu.VMEM((4, cycles, SUB, LANE), F32),
            pltpu.VMEM((4, 2, 4, 4, 2, SUB, LANE), F32),
            pltpu.VMEM((2, 4, 4, 2, SUB, border * LANE), F32),
            pltpu.VMEM((WIDTH, WIDTH), F32),
            pltpu.VMEM((LANE, LANE), F32),
            pltpu.VMEM((LANE, WIDTH), F32),
            pltpu.VMEM((cycles * CHILDREN * SUB, WIDTH), F32),
            pltpu.VMEM((cycles * CHILDREN * SUB, WIDTH), F32),
            pltpu.SemaphoreType.DMA((3,)),
            *(pltpu.SemaphoreType.DMA((n,)) for n in counts for _ in range(2)),
        ],
        compiler_params=pltpu.CompilerParams(collective_id=0, has_side_effects=True),
        name="fronts",
    )(
        border_map,
        child_front.reshape(cycles * CHILDREN * SUB * cycles, LANE),
        parent_front.reshape(cycles * SUB * cycles, LANE),
    )
    child_factor, parent_factor, tail = pl.pallas_call(
        hand_on,
        out_shape=tuple(
            jax.ShapeDtypeStruct(value.shape, F32) for value in (child_factor, parent_factor, tail)
        ),
        in_specs=[vmem] * 3,
        out_specs=(vmem,) * 3,
        name="hand_on",
    )(child_factor, parent_factor, tail)
    return (
        child_factor.reshape(1, cycles, 1, CHILDREN, SUB, 1, 1, LANE),
        parent_factor.reshape(cycles, 1, 1, SUB, 1, 1, LANE),
        tail.reshape(border, 1, 1, SUB, border, 1, LANE),
    )


def solution(mesh):
    return jax.shard_map(
        shards,
        mesh=mesh,
        in_specs=(
            P("cube", None, "row", None, None, None, "col", None),
            P(None, "row", "cube", None, None, "col", None),
            P(),
        ),
        out_specs=(
            P("cube", None, "row", None, None, None, "col", None),
            P(None, "row", "cube", None, None, "col", None),
            P(None, "row", "cube", None, None, "col", None),
        ),
        check_vma=False,
    )
```

```python
import functools

import jax
import jax.numpy as jnp
from jax import lax
from jax.experimental import pallas as pl
from jax.experimental.pallas import tpu as pltpu
from jax.sharding import PartitionSpec as P

CHILDREN = 2
SUB = 8
LANE = 128
WIDTH = 512
STEP = 8
HIGHEST = lax.Precision.HIGHEST
MESH = pl.DeviceIdType.MESH
F32 = jnp.float32


def mm(a, b):
    return jnp.dot(a, b, precision=HIGHEST, preferred_element_type=F32)


def mm_t(a, b):
    return lax.dot_general(
        a, b, (((1,), (1,)), ((), ())), precision=HIGHEST, preferred_element_type=F32
    )


def diagonal_inverse(tiles, out_ref, midway):
    rows = list(tiles)
    lane = lax.broadcasted_iota(jnp.int32, (SUB, LANE), 1)
    n = LANE // SUB

    def across_lanes(tile, index):
        picks = jnp.full((SUB, LANE), index, jnp.int32)
        return jnp.take_along_axis(tile, picks, axis=1, mode="promise_in_bounds")

    def across_rows(tile, index):
        return jnp.broadcast_to(tile[index : index + 1, :], (SUB, LANE))

    for t in range(n):
        j = t * SUB
        if t == n // 2:
            midway()
        inside = (lane >= j) & (lane < j + STEP)
        near = range(t + 1, min(n, t + 2))
        column = [across_lanes(rows[t], j + a) for a in range(STEP)]
        below = {i: [across_lanes(rows[i], j + a) for a in range(STEP)] for i in near}
        rest = {i: jnp.where(inside, 0.0, rows[i]) for i in range(t + 1, n)}
        right = [
            jnp.where(lane == j + a, 1.0, jnp.where(inside, 0.0, across_rows(rows[t], a)))
            for a in range(STEP)
        ]
        pivot = {
            (a, b): across_rows(column[b], a) for a in range(STEP) for b in range(a, STEP)
        }
        scaled, ratio = [], {}
        for a in range(STEP):
            inverse = 1.0 / pivot[a, a]
            scaled.append(right[a] * inverse)
            row = jnp.where(lane <= j + a, right[a] * lax.rsqrt(pivot[a, a]), 0.0)
            out_ref[j + a : j + a + 1, :] = row[:1, :]
            for b in range(a + 1, STEP):
                ratio[a, b] = pivot[a, b] * inverse
                for d in range(b, STEP):
                    pivot[b, d] = pivot[b, d] - ratio[a, b] * pivot[a, d]
                right[b] = right[b] - pivot[a, b] * scaled[a]
                for i in near:
                    below[i][b] = below[i][b] - below[i][a] * ratio[a, b]
            for i in near:
                rest[i] = rest[i] - below[i][a] * scaled[a]
        if t + 2 < n:
            for b in range(STEP - 1, 0, -1):
                for a in range(b):
                    scaled[a] = scaled[a] - ratio[a, b] * scaled[b]
        for i in range(t + 2, n):
            for a in range(STEP):
                rest[i] = rest[i] - across_lanes(rows[i], j + a) * scaled[a]
        for i in range(t + 1, n):
            rows[i] = rest[i]


def inverse_factor(matrix, block, strip, low, midway, after):
    blocks = WIDTH // LANE
    low[...] = jnp.zeros(low.shape, F32)
    strip[...] = jnp.zeros(strip.shape, F32)

    def body(k, carry):
        here = pl.ds(pl.multiple_of(k * LANE, LANE), LANE)
        share = matrix[here, here] - mm(low[here, :], strip[:, here])
        tiles = [share[SUB * i : SUB * (i + 1), :] for i in range(LANE // SUB)]
        for i in range(1, blocks):
            below = slice(i * LANE, (i + 1) * LANE)
            matrix[below, :] = matrix[below, :] - mm(low[below, :], strip[...])
        diagonal_inverse(tiles, block, lambda: midway(k))
        after(k)
        strip[...] = mm(block[...], matrix[here, :])
        strip[:, here] = block[...]
        for i in range(1, blocks):
            below = slice(i * LANE, (i + 1) * LANE)
            low[below, :] = jnp.where(k < i, mm_t(matrix[below, here], block[...]), 0.0)
            matrix[below, here] = jnp.where(k < i, 0.0, matrix[below, here])
        for i in range(blocks):
            columns = slice(i * LANE, (i + 1) * LANE)
            matrix[here, columns] = jnp.where(k >= i, strip[:, columns], 0.0)
        return carry

    lax.fori_loop(0, blocks, body, 0)


class Sends:
    def __init__(self, send, recv):
        self.send, self.recv, self.copies = send, recv, []

    def add(self, src, dst, device):
        index = len(self.copies)
        copy = pltpu.make_async_remote_copy(
            src_ref=src,
            dst_ref=dst,
            send_sem=self.send.at[index],
            recv_sem=self.recv.at[index],
            device_id=device,
            device_id_type=MESH,
        )
        self.copies.append(copy)

    def start(self):
        for copy in self.copies:
            copy.start()

    def arrived(self):
        for copy in self.copies:
            copy.wait_recv()

    def left(self):
        for copy in self.copies:
            copy.wait_send()


def greet(peers):
    barrier = pltpu.get_barrier_semaphore()
    for device in peers:
        pl.semaphore_signal(barrier, inc=1, device_id=device, device_id_type=MESH)
    pl.semaphore_wait(barrier, len(peers))


def fill(matrix, corner, first, last):
    for i in range(first, last):
        matrix[:, i * LANE : (i + 1) * LANE] = corner[i].reshape(WIDTH, LANE)


class Panel:
    def __init__(self, corner, across, near, line, xs, other, own, band, late, sems):
        self.late = late
        self.corner, self.across = corner, across
        self.near, self.line, self.xs, self.other = near, line, xs, other
        self.own, self.band = own, band
        (self.dz, self.dx0, self.dx1, self.dc0, self.dc1, self.az, self.ring, self.on, self.ac) = (
            Sends(*pair) for pair in sems
        )

    def stages(self):
        return (
            self.dz, self.dx0, self.dx1, self.dc0, self.dc1, self.az, self.ring, self.on, self.ac
        )

    def corner_out(self, tile):
        for device in self.near:
            self.dz.add(tile, self.own(self.corner), device)
        self.dz.start()

    def across_out(self, strip):
        for device in self.line:
            self.az.add(strip, self.band(self.across), device)
        if not self.late:
            self.az.start()

    def corner_on(self, along_x, along_core):
        self.dz.arrived()
        for stage, part in ((self.dx0, slice(0, 1)), (self.dx1, slice(1, 4))):
            piece = along_x(self.corner, part)
            for device in self.xs:
                stage.add(piece, piece, device)
            stage.start()
        for stage, part in ((self.dc0, slice(0, 1)), (self.dc1, slice(1, 4))):
            piece = along_core(self.corner, part)
            stage.add(piece, piece, self.other)
        if self.late:
            self.az.start()
        self.dx0.arrived()
        self.dc0.start()

    def prepare_across(self, x, block):
        cut = self.across.shape[-1] // 2 // LANE * LANE
        half = (slice(0, cut), slice(cut, None))
        right, left = self.xs[0], self.xs[2]
        for device, part in ((right, 0), (left, 1), (right, 1), (left, 0)):
            piece = block(x, half[part])
            self.ring.add(piece, piece, device)
        piece = block((x + 3) % 4, half[0])
        self.on.add(piece, piece, right)
        piece = block((x + 1) % 4, half[1])
        self.on.add(piece, piece, left)
        for d in (0, 1, 3, 2):
            piece = block((x + d) % 4, slice(None))
            self.ac.add(piece, piece, self.other)

    def factor(self, matrix, block, strip, low, also):
        self.dc0.arrived()
        fill(matrix, self.corner, 0, 1)

        def midway(k):
            @pl.when(k == 0)
            def _():
                self.dx1.arrived()
                self.dc1.start()
                if not self.late:
                    self.az.arrived()
                    self.ring.start()
                also()

            @pl.when(k == 3)
            def _():
                self.on.arrived()
                self.ac.copies[3].start()

        def after(k):
            @pl.when(k == 0)
            def _():
                if self.late:
                    self.az.arrived()
                    self.ring.start()
                self.dc1.arrived()
                fill(matrix, self.corner, 1, 4)

            @pl.when(k == 1)
            def _():
                for copy in self.ring.copies[:2]:
                    copy.wait_recv()
                self.on.start()

            @pl.when(k == 2)
            def _():
                for copy in self.ring.copies[2:]:
                    copy.wait_recv()
                for copy in self.ac.copies[:3]:
                    copy.start()

        inverse_factor(matrix, block, strip, low, midway, after)


def kernel(
    border_map, child_hbm, parent_hbm, child_factor, parent_factor, tail,
    child_in, parent_in, front, c_panel, c_corner, c_across, update,
    taken, total, p_panel, p_corner, p_across,
    matrix, block, strip, low, wide, whole, local, *sems,
):
    cube, row, col = lax.axis_index("cube"), lax.axis_index("row"), lax.axis_index("col")
    core, zl, child = cube % 2, cube // 2, cube // 4
    half = zl % 2
    x, zh = row % 4, row // 4
    cycles = front.shape[0]
    border = cycles - 1
    width = border * LANE

    def at(dz, dh, dy):
        return ((zl + dz) % 4 * 2 + core, (zh + dh) % 2 * 4 + x, (col + dy) % 4)

    def at_half(dz, dh, dy):
        return (child * 4 + (half + dz) % 2 * 2 + core, (zh + dh) % 2 * 4 + x, (col + dy) % 4)

    c_near = [at_half(a, b, d) for a in range(2) for b in range(2) for d in range(4) if a + b + d]
    p_near = [at(a, b, d) for a in range(4) for b in range(2) for d in range(4) if a + b + d]
    c_line = [at_half(a, b, 0) for a in range(2) for b in range(2) if a + b]
    p_line = [at(a, b, 0) for a in range(4) for b in range(2) if a + b]
    ys = [at(0, 0, d) for d in (1, 2, 3)]
    xs = [(cube, zh * 4 + (x + d) % 4, col) for d in (1, 2, 3)]
    other = (cube + 1 - 2 * core, row, col)
    partner = ((cube + 4) % 8, row, col)
    pairs_of = [(sems[2 * i], sems[2 * i + 1]) for i in range(len(sems) // 2)]
    def lay(t):
        for h in range(CHILDREN):
            for s in range(cycles):
                start = ((t * CHILDREN + h) * SUB) * cycles + s
                front[t, h, :, s * LANE : (s + 1) * LANE] = child_in[
                    pl.ds(start, SUB, stride=cycles), :
                ]

    head = CHILDREN * SUB * cycles
    loads = [
        pltpu.make_async_copy(child_hbm.at[:head], child_in.at[:head], local.at[0]),
        pltpu.make_async_copy(child_hbm.at[head:], child_in.at[head:], local.at[1]),
        pltpu.make_async_copy(parent_hbm, parent_in, local.at[2]),
    ]
    for load in loads:
        load.start()
    loads[0].wait()
    lay(0)
    greet(p_near + xs + [other])

    child_side = Panel(
        c_corner, c_across, c_near, c_line, xs, other,
        lambda ref: ref.at[col, zh, x, :, half, core],
        lambda ref: ref.at[zh, x, :, half, core],
        True, pairs_of[0:9],
    )
    child_side.corner_out(front.at[0, :, :, 0:LANE])
    child_side.across_out(front.at[0, :, :, LANE:])
    own = front[0]
    c_corner[pl.ds(col, 1), pl.ds(zh, 1), pl.ds(x, 1), :, pl.ds(half, 1), pl.ds(core, 1)] = own[
        :, :, 0:LANE
    ].reshape(1, 1, 1, CHILDREN, 1, 1, SUB, LANE)
    c_across[pl.ds(zh, 1), pl.ds(x, 1), :, pl.ds(half, 1), pl.ds(core, 1)] = own[
        :, :, LANE:
    ].reshape(1, 1, CHILDREN, 1, 1, SUB, width)
    loads[1].wait()
    for t in range(1, cycles):
        lay(t)
    loads[2].wait()
    c_rest = Sends(*pairs_of[18])
    for device in ys:
        c_rest.add(front.at[:, :, :, 0:LANE], c_panel.at[col], device)
    c_rest.start()
    c_panel[pl.ds(col, 1)] = front[:, :, :, 0:LANE][None]
    child_side.corner_on(
        lambda ref, part: ref.at[part, :, x, :, :, core],
        lambda ref, part: ref.at[part, :, :, :, :, core],
    )
    child_side.prepare_across(x, lambda at_x, part: c_across.at[:, at_x, :, :, core, :, part])
    child_side.factor(matrix, block, strip, low, lambda: None)

    c_rest.arrived()
    for i in range(4):
        wide[:, i * LANE : (i + 1) * LANE] = c_panel[i].reshape(cycles * CHILDREN * SUB, LANE)
    whole[...] = mm_t(wide[...], matrix[...])
    wide[...] = mm(whole[...], matrix[...])
    child_side.ac.arrived()

    def child_update(first, last, begin, end):
        for left in range(begin, end, 2 * LANE):
            size = min(2 * LANE, end - left)
            product = mm(
                wide[(first + 1) * CHILDREN * SUB : (last + 1) * CHILDREN * SUB, :],
                c_across[:, :, :, :, :, :, left : left + size].reshape(WIDTH, size),
            ).reshape(last - first, CHILDREN, SUB, size)
            for h in range(CHILDREN):
                update[h, first:last, :, left : left + size] = (
                    front[first + 1 : last + 1, h, :, LANE + left : LANE + left + size]
                    - product[:, h]
                )

    sibling = Sends(*pairs_of[19])
    for rows, columns in (
        (slice(0, 1), slice(0, LANE)),
        (slice(0, 1), slice(LANE, None)),
        (slice(1, None), slice(0, LANE)),
        (slice(1, None), slice(LANE, None)),
    ):
        sibling.add(
            update.at[1 - child, rows, :, columns], taken.at[rows, :, columns], partner
        )
    child_update(0, 1, 0, LANE)
    sibling.copies[0].start()
    child_update(0, 1, LANE, width)
    sibling.copies[1].start()
    child_update(1, border, 0, LANE)
    sibling.copies[2].start()

    holes = []
    for index in (child, 1 - child):
        hole = cycles * (cycles - 1) // 2
        for i in range(border):
            hole = hole - border_map[index, i]
        holes.append(hole)

    def shifted(pick, hole, p):
        if p == 0:
            return jnp.where(hole > 0, pick(0), 0.0)
        if p == border:
            return jnp.where(hole < p, pick(p - 1), 0.0)
        return jnp.where(hole > p, pick(p), jnp.where(hole < p, pick(p - 1), 0.0))

    sources = (
        lambda i, j: update[child, i, :, j * LANE : (j + 1) * LANE],
        lambda i, j: taken[i, :, j * LANE : (j + 1) * LANE],
    )

    def assemble(p, q):
        value = parent_in[pl.ds(p * SUB * cycles + q, SUB, stride=cycles), :]
        for source, hole in zip(sources, holes):
            value = value + shifted(lambda i: shifted(lambda j: source(i, j), hole, q), hole, p)
        total[p, :, q * LANE : (q + 1) * LANE] = value

    parent_side = Panel(
        p_corner, p_across, p_near, p_line, xs, other,
        lambda ref: ref.at[col, zh, x, zl, core],
        lambda ref: ref.at[zh, x, zl, core],
        False, pairs_of[9:18],
    )
    sibling.copies[0].wait_recv()
    assemble(0, 0)
    parent_side.corner_out(total.at[0, :, 0:LANE])
    sibling.copies[1].wait_recv()
    for q in range(1, cycles):
        assemble(0, q)
    parent_side.across_out(total.at[0, :, LANE:])
    own = total[0]
    p_corner[pl.ds(col, 1), pl.ds(zh, 1), pl.ds(x, 1), pl.ds(zl, 1), pl.ds(core, 1)] = own[
        :, 0:LANE
    ].reshape(1, 1, 1, 1, 1, SUB, LANE)
    p_across[pl.ds(zh, 1), pl.ds(x, 1), pl.ds(zl, 1), pl.ds(core, 1)] = own[:, LANE:].reshape(
        1, 1, 1, 1, SUB, width
    )
    sibling.copies[2].wait_recv()
    for p in range(1, cycles):
        assemble(p, 0)
    p_rest = Sends(*pairs_of[20])
    for device in ys:
        p_rest.add(total.at[:, :, 0:LANE], p_panel.at[col], device)
    p_rest.start()
    p_panel[pl.ds(col, 1)] = total[:, :, 0:LANE][None]
    child_update(1, border, LANE, width)
    child_factor[...] = whole[:, pl.ds(pl.multiple_of(col * LANE, LANE), LANE)]
    parent_side.corner_on(
        lambda ref, part: ref.at[part, :, x, :, core],
        lambda ref, part: ref.at[part, :, :, :, core],
    )
    parent_side.prepare_across(x, lambda at_x, part: p_across.at[:, at_x, :, core, :, part])
    parent_side.factor(matrix, block, strip, low, lambda: sibling.copies[3].start())

    p_rest.arrived()
    rows = cycles * SUB
    for i in range(4):
        wide[:rows, i * LANE : (i + 1) * LANE] = p_panel[i].reshape(rows, LANE)
    whole[:rows, :] = mm_t(wide[:rows, :], matrix[...])
    wide[:rows, :] = mm(whole[:rows, :], matrix[...])
    parent_factor[...] = whole[:rows, pl.ds(pl.multiple_of(col * LANE, LANE), LANE)]
    sibling.copies[3].wait_recv()
    for p in range(1, cycles):
        for q in range(1, cycles):
            assemble(p, q)
    parent_side.ac.arrived()
    for left in range(0, width, 2 * LANE):
        size = min(2 * LANE, width - left)
        product = mm(
            wide[SUB:rows, :], p_across[:, :, :, :, :, left : left + size].reshape(WIDTH, size)
        ).reshape(border, SUB, size)
        value = total[1:, :, LANE + left : LANE + left + size] - product
        for p in range(border):
            for q in range(size // LANE):
                tail[pl.ds(p * SUB * border + left // LANE + q, SUB, stride=border), :] = value[
                    p, :, q * LANE : (q + 1) * LANE
                ]
    for stage in (*child_side.stages(), *parent_side.stages(), c_rest, sibling, p_rest):
        stage.left()


def hand_on(first, second, third, first_out, second_out, third_out):
    first_out[...] = first[...]
    second_out[...] = second[...]
    third_out[...] = third[...]


def shards(child_front, parent_front, border_map):
    cycles = child_front.shape[1]
    border = cycles - 1
    vmem = pl.BlockSpec(memory_space=pltpu.VMEM)
    smem = pl.BlockSpec(memory_space=pltpu.SMEM)
    kept = pl.BlockSpec(memory_space=pl.ANY)
    counts = [15, 3, 3, 1, 1, 3, 4, 2, 4, 31, 3, 3, 1, 1, 7, 4, 2, 4, 3, 4, 3]
    child_factor, parent_factor, tail = pl.pallas_call(
        kernel,
        out_shape=(
            jax.ShapeDtypeStruct((cycles * CHILDREN * SUB, LANE), F32),
            jax.ShapeDtypeStruct((cycles * SUB, LANE), F32),
            jax.ShapeDtypeStruct((border * SUB * border, LANE), F32),
        ),
        in_specs=[smem, kept, kept],
        out_specs=(vmem, vmem, vmem),
        scratch_shapes=[
            pltpu.VMEM((cycles * CHILDREN * SUB * cycles, LANE), F32),
            pltpu.VMEM((cycles * SUB * cycles, LANE), F32),
            pltpu.VMEM((cycles, CHILDREN, SUB, cycles * LANE), F32),
            pltpu.VMEM((4, cycles, CHILDREN, SUB, LANE), F32),
            pltpu.VMEM((4, 2, 4, CHILDREN, 2, 2, SUB, LANE), F32),
            pltpu.VMEM((2, 4, CHILDREN, 2, 2, SUB, border * LANE), F32),
            pltpu.VMEM((CHILDREN, border, SUB, border * LANE), F32),
            pltpu.VMEM((border, SUB, border * LANE), F32),
            pltpu.VMEM((cycles, SUB, cycles * LANE), F32),
            pltpu.VMEM((4, cycles, SUB, LANE), F32),
            pltpu.VMEM((4, 2, 4, 4, 2, SUB, LANE), F32),
            pltpu.VMEM((2, 4, 4, 2, SUB, border * LANE), F32),
            pltpu.VMEM((WIDTH, WIDTH), F32),
            pltpu.VMEM((LANE, LANE), F32),
            pltpu.VMEM((LANE, WIDTH), F32),
            pltpu.VMEM((WIDTH, LANE), F32),
            pltpu.VMEM((cycles * CHILDREN * SUB, WIDTH), F32),
            pltpu.VMEM((cycles * CHILDREN * SUB, WIDTH), F32),
            pltpu.SemaphoreType.DMA((3,)),
            *(pltpu.SemaphoreType.DMA((n,)) for n in counts for _ in range(2)),
        ],
        compiler_params=pltpu.CompilerParams(collective_id=0, has_side_effects=True),
        name="fronts",
    )(
        border_map,
        child_front.reshape(cycles * CHILDREN * SUB * cycles, LANE),
        parent_front.reshape(cycles * SUB * cycles, LANE),
    )
    child_factor, parent_factor, tail = pl.pallas_call(
        hand_on,
        out_shape=tuple(
            jax.ShapeDtypeStruct(value.shape, F32) for value in (child_factor, parent_factor, tail)
        ),
        in_specs=[vmem] * 3,
        out_specs=(vmem,) * 3,
        name="hand_on",
    )(child_factor, parent_factor, tail)
    return (
        child_factor.reshape(1, cycles, 1, CHILDREN, SUB, 1, 1, LANE),
        parent_factor.reshape(cycles, 1, 1, SUB, 1, 1, LANE),
        tail.reshape(border, 1, 1, SUB, border, 1, LANE),
    )


def solution(mesh):
    return jax.shard_map(
        shards,
        mesh=mesh,
        in_specs=(
            P("cube", None, "row", None, None, None, "col", None),
            P(None, "row", "cube", None, None, "col", None),
            P(),
        ),
        out_specs=(
            P("cube", None, "row", None, None, None, "col", None),
            P(None, "row", "cube", None, None, "col", None),
            P(None, "row", "cube", None, None, "col", None),
        ),
        check_vma=False,
    )
```

```python
import functools

import jax
import jax.numpy as jnp
from jax import lax
from jax.experimental import pallas as pl
from jax.experimental.pallas import tpu as pltpu
from jax.sharding import PartitionSpec as P

CHILDREN = 2
SUB = 8
LANE = 128
WIDTH = 512
STEP = 8
HIGHEST = lax.Precision.HIGHEST
MESH = pl.DeviceIdType.MESH
F32 = jnp.float32


def mm(a, b):
    return jnp.dot(a, b, precision=HIGHEST, preferred_element_type=F32)


def mm_t(a, b):
    return lax.dot_general(
        a, b, (((1,), (1,)), ((), ())), precision=HIGHEST, preferred_element_type=F32
    )


def diagonal_inverse(tiles, out_ref, midway):
    rows = list(tiles)
    lane = lax.broadcasted_iota(jnp.int32, (SUB, LANE), 1)
    n = LANE // SUB

    def across_lanes(tile, index):
        picks = jnp.full((SUB, LANE), index, jnp.int32)
        return jnp.take_along_axis(tile, picks, axis=1, mode="promise_in_bounds")

    def across_rows(tile, index):
        return jnp.broadcast_to(tile[index : index + 1, :], (SUB, LANE))

    for t in range(n):
        j = t * SUB
        if t == n // 2:
            midway()
        inside = (lane >= j) & (lane < j + STEP)
        near = range(t + 1, min(n, t + 2))
        column = [across_lanes(rows[t], j + a) for a in range(STEP)]
        below = {i: [across_lanes(rows[i], j + a) for a in range(STEP)] for i in near}
        rest = {i: jnp.where(inside, 0.0, rows[i]) for i in range(t + 1, n)}
        right = [
            jnp.where(lane == j + a, 1.0, jnp.where(inside, 0.0, across_rows(rows[t], a)))
            for a in range(STEP)
        ]
        pivot = {
            (a, b): across_rows(column[b], a) for a in range(STEP) for b in range(a, STEP)
        }
        scaled, ratio = [], {}
        for a in range(STEP):
            inverse = 1.0 / pivot[a, a]
            scaled.append(right[a] * inverse)
            row = jnp.where(lane <= j + a, right[a] * lax.rsqrt(pivot[a, a]), 0.0)
            out_ref[j + a : j + a + 1, :] = row[:1, :]
            for b in range(a + 1, STEP):
                ratio[a, b] = pivot[a, b] * inverse
                for d in range(b, STEP):
                    pivot[b, d] = pivot[b, d] - ratio[a, b] * pivot[a, d]
                right[b] = right[b] - pivot[a, b] * scaled[a]
                for i in near:
                    below[i][b] = below[i][b] - below[i][a] * ratio[a, b]
            for i in near:
                rest[i] = rest[i] - below[i][a] * scaled[a]
        if t + 2 < n:
            for b in range(STEP - 1, 0, -1):
                for a in range(b):
                    scaled[a] = scaled[a] - ratio[a, b] * scaled[b]
        for i in range(t + 2, n):
            for a in range(STEP):
                rest[i] = rest[i] - across_lanes(rows[i], j + a) * scaled[a]
        for i in range(t + 1, n):
            rows[i] = rest[i]


def inverse_factor(matrix, block, strip, low, midway, after):
    blocks = WIDTH // LANE
    for k in range(blocks):
        here = slice(k * LANE, (k + 1) * LANE)
        share = matrix[here, here]
        if k:
            share = share - mm(low[here, :], strip[:, here])
        tiles = [share[SUB * i : SUB * (i + 1), :] for i in range(LANE // SUB)]
        for i in range(k, blocks) if k else ():
            below = slice(i * LANE, (i + 1) * LANE)
            matrix[below, :] = matrix[below, :] - mm(low[below, :], strip[...])
        diagonal_inverse(tiles, block, lambda: midway(k))
        after(k)
        strip[...] = mm(block[...], matrix[here, :])
        strip[:, here] = block[...]
        for i in range(k + 1, blocks):
            below = slice(i * LANE, (i + 1) * LANE)
            low[below, :] = mm_t(matrix[below, here], block[...])
            matrix[below, here] = jnp.zeros((LANE, LANE), F32)
        for i in range(blocks):
            columns = slice(i * LANE, (i + 1) * LANE)
            if k >= i:
                matrix[here, columns] = strip[:, columns]
            else:
                matrix[here, columns] = jnp.zeros((LANE, LANE), F32)


def only(chosen):
    def run(action):
        if chosen:
            action()

    return run


class Sends:
    def __init__(self, send, recv):
        self.send, self.recv, self.copies = send, recv, []

    def add(self, src, dst, device):
        index = len(self.copies)
        copy = pltpu.make_async_remote_copy(
            src_ref=src,
            dst_ref=dst,
            send_sem=self.send.at[index],
            recv_sem=self.recv.at[index],
            device_id=device,
            device_id_type=MESH,
        )
        self.copies.append(copy)

    def start(self):
        for copy in self.copies:
            copy.start()

    def arrived(self):
        for copy in self.copies:
            copy.wait_recv()

    def left(self):
        for copy in self.copies:
            copy.wait_send()


def greet(peers):
    barrier = pltpu.get_barrier_semaphore()
    for device in peers:
        pl.semaphore_signal(barrier, inc=1, device_id=device, device_id_type=MESH)
    pl.semaphore_wait(barrier, len(peers))


def fill(matrix, corner, first, last):
    for i in range(first, last):
        matrix[:, i * LANE : (i + 1) * LANE] = corner[i].reshape(WIDTH, LANE)


class Panel:
    def __init__(self, corner, across, near, line, xs, other, own, band, late, sems):
        self.late = late
        self.corner, self.across = corner, across
        self.near, self.line, self.xs, self.other = near, line, xs, other
        self.own, self.band = own, band
        (self.dz, self.dx0, self.dx1, self.dc0, self.dc1, self.az, self.ring, self.on, self.ac) = (
            Sends(*pair) for pair in sems
        )

    def stages(self):
        return (
            self.dz, self.dx0, self.dx1, self.dc0, self.dc1, self.az, self.ring, self.on, self.ac
        )

    def corner_out(self, tile):
        for device in self.near:
            self.dz.add(tile, self.own(self.corner), device)
        self.dz.start()

    def across_out(self, strip):
        for device in self.line:
            self.az.add(strip, self.band(self.across), device)
        if not self.late:
            self.az.start()

    def corner_on(self, along_x, along_core):
        self.dz.arrived()
        for stage, part in ((self.dx0, slice(0, 1)), (self.dx1, slice(1, 4))):
            piece = along_x(self.corner, part)
            for device in self.xs:
                stage.add(piece, piece, device)
            stage.start()
        for stage, part in ((self.dc0, slice(0, 1)), (self.dc1, slice(1, 4))):
            piece = along_core(self.corner, part)
            stage.add(piece, piece, self.other)
        if self.late:
            self.az.start()
        self.dx0.arrived()
        self.dc0.start()

    def prepare_across(self, x, block):
        cut = self.across.shape[-1] // 2 // LANE * LANE
        half = (slice(0, cut), slice(cut, None))
        right, left = self.xs[0], self.xs[2]
        for device, part in ((right, 0), (left, 1), (right, 1), (left, 0)):
            piece = block(x, half[part])
            self.ring.add(piece, piece, device)
        piece = block((x + 3) % 4, half[0])
        self.on.add(piece, piece, right)
        piece = block((x + 1) % 4, half[1])
        self.on.add(piece, piece, left)
        for d in (0, 1, 3, 2):
            piece = block((x + d) % 4, slice(None))
            self.ac.add(piece, piece, self.other)

    def factor(self, matrix, block, strip, low, also):
        self.dc0.arrived()
        fill(matrix, self.corner, 0, 1)

        def midway(k):
            @only(k == 0)
            def _():
                self.dx1.arrived()
                self.dc1.start()
                if not self.late:
                    self.az.arrived()
                    self.ring.start()
                also()

            @only(k == 3)
            def _():
                self.on.arrived()
                self.ac.copies[3].start()

        def after(k):
            @only(k == 0)
            def _():
                if self.late:
                    self.az.arrived()
                    self.ring.start()
                self.dc1.arrived()
                fill(matrix, self.corner, 1, 4)

            @only(k == 1)
            def _():
                for copy in self.ring.copies[:2]:
                    copy.wait_recv()
                self.on.start()

            @only(k == 2)
            def _():
                for copy in self.ring.copies[2:]:
                    copy.wait_recv()
                for copy in self.ac.copies[:3]:
                    copy.start()

        inverse_factor(matrix, block, strip, low, midway, after)


def kernel(
    border_map, child_hbm, parent_hbm, child_factor, parent_factor, tail,
    child_in, parent_in, front, c_panel, c_corner, c_across, update,
    taken, total, p_panel, p_corner, p_across,
    matrix, block, strip, low, wide, whole, local, *sems,
):
    cube, row, col = lax.axis_index("cube"), lax.axis_index("row"), lax.axis_index("col")
    core, zl, child = cube % 2, cube // 2, cube // 4
    half = zl % 2
    x, zh = row % 4, row // 4
    cycles = front.shape[0]
    border = cycles - 1
    width = border * LANE

    def at(dz, dh, dy):
        return ((zl + dz) % 4 * 2 + core, (zh + dh) % 2 * 4 + x, (col + dy) % 4)

    def at_half(dz, dh, dy):
        return (child * 4 + (half + dz) % 2 * 2 + core, (zh + dh) % 2 * 4 + x, (col + dy) % 4)

    c_near = [at_half(a, b, d) for a in range(2) for b in range(2) for d in range(4) if a + b + d]
    p_near = [at(a, b, d) for a in range(4) for b in range(2) for d in range(4) if a + b + d]
    c_line = [at_half(a, b, 0) for a in range(2) for b in range(2) if a + b]
    p_line = [at(a, b, 0) for a in range(4) for b in range(2) if a + b]
    ys = [at(0, 0, d) for d in (1, 2, 3)]
    xs = [(cube, zh * 4 + (x + d) % 4, col) for d in (1, 2, 3)]
    other = (cube + 1 - 2 * core, row, col)
    partner = ((cube + 4) % 8, row, col)
    pairs_of = [(sems[2 * i], sems[2 * i + 1]) for i in range(len(sems) // 2)]
    def lay(t):
        for h in range(CHILDREN):
            for s in range(cycles):
                start = ((t * CHILDREN + h) * SUB) * cycles + s
                front[t, h, :, s * LANE : (s + 1) * LANE] = child_in[
                    pl.ds(start, SUB, stride=cycles), :
                ]

    head = CHILDREN * SUB * cycles
    loads = [
        pltpu.make_async_copy(child_hbm.at[:head], child_in.at[:head], local.at[0]),
        pltpu.make_async_copy(child_hbm.at[head:], child_in.at[head:], local.at[1]),
        pltpu.make_async_copy(parent_hbm, parent_in, local.at[2]),
    ]
    for load in loads:
        load.start()
    loads[0].wait()
    lay(0)
    greet(p_near + xs + [other])

    child_side = Panel(
        c_corner, c_across, c_near, c_line, xs, other,
        lambda ref: ref.at[col, zh, x, :, half, core],
        lambda ref: ref.at[zh, x, :, half, core],
        True, pairs_of[0:9],
    )
    child_side.corner_out(front.at[0, :, :, 0:LANE])
    child_side.across_out(front.at[0, :, :, LANE:])
    own = front[0]
    c_corner[pl.ds(col, 1), pl.ds(zh, 1), pl.ds(x, 1), :, pl.ds(half, 1), pl.ds(core, 1)] = own[
        :, :, 0:LANE
    ].reshape(1, 1, 1, CHILDREN, 1, 1, SUB, LANE)
    c_across[pl.ds(zh, 1), pl.ds(x, 1), :, pl.ds(half, 1), pl.ds(core, 1)] = own[
        :, :, LANE:
    ].reshape(1, 1, CHILDREN, 1, 1, SUB, width)
    loads[1].wait()
    for t in range(1, cycles):
        lay(t)
    loads[2].wait()
    c_rest = Sends(*pairs_of[18])
    for device in ys:
        c_rest.add(front.at[:, :, :, 0:LANE], c_panel.at[col], device)
    c_rest.start()
    c_panel[pl.ds(col, 1)] = front[:, :, :, 0:LANE][None]
    child_side.corner_on(
        lambda ref, part: ref.at[part, :, x, :, :, core],
        lambda ref, part: ref.at[part, :, :, :, :, core],
    )
    child_side.prepare_across(x, lambda at_x, part: c_across.at[:, at_x, :, :, core, :, part])
    child_side.factor(matrix, block, strip, low, lambda: None)

    c_rest.arrived()
    for i in range(4):
        wide[:, i * LANE : (i + 1) * LANE] = c_panel[i].reshape(cycles * CHILDREN * SUB, LANE)
    whole[...] = mm_t(wide[...], matrix[...])
    wide[...] = mm(whole[...], matrix[...])
    child_side.ac.arrived()

    def child_update(first, last, begin, end):
        for left in range(begin, end, 2 * LANE):
            size = min(2 * LANE, end - left)
            product = mm(
                wide[(first + 1) * CHILDREN * SUB : (last + 1) * CHILDREN * SUB, :],
                c_across[:, :, :, :, :, :, left : left + size].reshape(WIDTH, size),
            ).reshape(last - first, CHILDREN, SUB, size)
            for h in range(CHILDREN):
                update[h, first:last, :, left : left + size] = (
                    front[first + 1 : last + 1, h, :, LANE + left : LANE + left + size]
                    - product[:, h]
                )

    sibling = Sends(*pairs_of[19])
    for rows, columns in (
        (slice(0, 1), slice(0, LANE)),
        (slice(0, 1), slice(LANE, None)),
        (slice(1, None), slice(0, LANE)),
        (slice(1, None), slice(LANE, None)),
    ):
        sibling.add(
            update.at[1 - child, rows, :, columns], taken.at[rows, :, columns], partner
        )
    child_update(0, 1, 0, LANE)
    sibling.copies[0].start()
    child_update(0, 1, LANE, width)
    sibling.copies[1].start()
    child_update(1, border, 0, LANE)
    sibling.copies[2].start()

    holes = []
    for index in (child, 1 - child):
        hole = cycles * (cycles - 1) // 2
        for i in range(border):
            hole = hole - border_map[index, i]
        holes.append(hole)

    def shifted(pick, hole, p):
        if p == 0:
            return jnp.where(hole > 0, pick(0), 0.0)
        if p == border:
            return jnp.where(hole < p, pick(p - 1), 0.0)
        return jnp.where(hole > p, pick(p), jnp.where(hole < p, pick(p - 1), 0.0))

    sources = (
        lambda i, j: update[child, i, :, j * LANE : (j + 1) * LANE],
        lambda i, j: taken[i, :, j * LANE : (j + 1) * LANE],
    )

    def assemble(p, q):
        value = parent_in[pl.ds(p * SUB * cycles + q, SUB, stride=cycles), :]
        for source, hole in zip(sources, holes):
            value = value + shifted(lambda i: shifted(lambda j: source(i, j), hole, q), hole, p)
        total[p, :, q * LANE : (q + 1) * LANE] = value

    parent_side = Panel(
        p_corner, p_across, p_near, p_line, xs, other,
        lambda ref: ref.at[col, zh, x, zl, core],
        lambda ref: ref.at[zh, x, zl, core],
        False, pairs_of[9:18],
    )
    sibling.copies[0].wait_recv()
    assemble(0, 0)
    parent_side.corner_out(total.at[0, :, 0:LANE])
    sibling.copies[1].wait_recv()
    for q in range(1, cycles):
        assemble(0, q)
    parent_side.across_out(total.at[0, :, LANE:])
    own = total[0]
    p_corner[pl.ds(col, 1), pl.ds(zh, 1), pl.ds(x, 1), pl.ds(zl, 1), pl.ds(core, 1)] = own[
        :, 0:LANE
    ].reshape(1, 1, 1, 1, 1, SUB, LANE)
    p_across[pl.ds(zh, 1), pl.ds(x, 1), pl.ds(zl, 1), pl.ds(core, 1)] = own[:, LANE:].reshape(
        1, 1, 1, 1, SUB, width
    )
    sibling.copies[2].wait_recv()
    for p in range(1, cycles):
        assemble(p, 0)
    p_rest = Sends(*pairs_of[20])
    for device in ys:
        p_rest.add(total.at[:, :, 0:LANE], p_panel.at[col], device)
    p_rest.start()
    p_panel[pl.ds(col, 1)] = total[:, :, 0:LANE][None]
    child_update(1, border, LANE, width)
    child_factor[...] = whole[:, pl.ds(pl.multiple_of(col * LANE, LANE), LANE)]
    parent_side.corner_on(
        lambda ref, part: ref.at[part, :, x, :, core],
        lambda ref, part: ref.at[part, :, :, :, core],
    )
    parent_side.prepare_across(x, lambda at_x, part: p_across.at[:, at_x, :, core, :, part])
    parent_side.factor(matrix, block, strip, low, lambda: sibling.copies[3].start())

    p_rest.arrived()
    rows = cycles * SUB
    for i in range(4):
        wide[:rows, i * LANE : (i + 1) * LANE] = p_panel[i].reshape(rows, LANE)
    whole[:rows, :] = mm_t(wide[:rows, :], matrix[...])
    wide[:rows, :] = mm(whole[:rows, :], matrix[...])
    parent_factor[...] = whole[:rows, pl.ds(pl.multiple_of(col * LANE, LANE), LANE)]
    sibling.copies[3].wait_recv()
    for p in range(1, cycles):
        for q in range(1, cycles):
            assemble(p, q)
    parent_side.ac.arrived()
    for left in range(0, width, 2 * LANE):
        size = min(2 * LANE, width - left)
        product = mm(
            wide[SUB:rows, :], p_across[:, :, :, :, :, left : left + size].reshape(WIDTH, size)
        ).reshape(border, SUB, size)
        value = total[1:, :, LANE + left : LANE + left + size] - product
        for p in range(border):
            for q in range(size // LANE):
                tail[pl.ds(p * SUB * border + left // LANE + q, SUB, stride=border), :] = value[
                    p, :, q * LANE : (q + 1) * LANE
                ]
    for stage in (*child_side.stages(), *parent_side.stages(), c_rest, sibling, p_rest):
        stage.left()


def hand_on(first, second, third, first_out, second_out, third_out):
    first_out[...] = first[...]
    second_out[...] = second[...]
    third_out[...] = third[...]


def shards(child_front, parent_front, border_map):
    cycles = child_front.shape[1]
    border = cycles - 1
    vmem = pl.BlockSpec(memory_space=pltpu.VMEM)
    smem = pl.BlockSpec(memory_space=pltpu.SMEM)
    kept = pl.BlockSpec(memory_space=pl.ANY)
    counts = [15, 3, 3, 1, 1, 3, 4, 2, 4, 31, 3, 3, 1, 1, 7, 4, 2, 4, 3, 4, 3]
    child_factor, parent_factor, tail = pl.pallas_call(
        kernel,
        out_shape=(
            jax.ShapeDtypeStruct((cycles * CHILDREN * SUB, LANE), F32),
            jax.ShapeDtypeStruct((cycles * SUB, LANE), F32),
            jax.ShapeDtypeStruct((border * SUB * border, LANE), F32),
        ),
        in_specs=[smem, kept, kept],
        out_specs=(vmem, vmem, vmem),
        scratch_shapes=[
            pltpu.VMEM((cycles * CHILDREN * SUB * cycles, LANE), F32),
            pltpu.VMEM((cycles * SUB * cycles, LANE), F32),
            pltpu.VMEM((cycles, CHILDREN, SUB, cycles * LANE), F32),
            pltpu.VMEM((4, cycles, CHILDREN, SUB, LANE), F32),
            pltpu.VMEM((4, 2, 4, CHILDREN, 2, 2, SUB, LANE), F32),
            pltpu.VMEM((2, 4, CHILDREN, 2, 2, SUB, border * LANE), F32),
            pltpu.VMEM((CHILDREN, border, SUB, border * LANE), F32),
            pltpu.VMEM((border, SUB, border * LANE), F32),
            pltpu.VMEM((cycles, SUB, cycles * LANE), F32),
            pltpu.VMEM((4, cycles, SUB, LANE), F32),
            pltpu.VMEM((4, 2, 4, 4, 2, SUB, LANE), F32),
            pltpu.VMEM((2, 4, 4, 2, SUB, border * LANE), F32),
            pltpu.VMEM((WIDTH, WIDTH), F32),
            pltpu.VMEM((LANE, LANE), F32),
            pltpu.VMEM((LANE, WIDTH), F32),
            pltpu.VMEM((WIDTH, LANE), F32),
            pltpu.VMEM((cycles * CHILDREN * SUB, WIDTH), F32),
            pltpu.VMEM((cycles * CHILDREN * SUB, WIDTH), F32),
            pltpu.SemaphoreType.DMA((3,)),
            *(pltpu.SemaphoreType.DMA((n,)) for n in counts for _ in range(2)),
        ],
        compiler_params=pltpu.CompilerParams(collective_id=0, has_side_effects=True),
        name="fronts",
    )(
        border_map,
        child_front.reshape(cycles * CHILDREN * SUB * cycles, LANE),
        parent_front.reshape(cycles * SUB * cycles, LANE),
    )
    child_factor, parent_factor, tail = pl.pallas_call(
        hand_on,
        out_shape=tuple(
            jax.ShapeDtypeStruct(value.shape, F32) for value in (child_factor, parent_factor, tail)
        ),
        in_specs=[vmem] * 3,
        out_specs=(vmem,) * 3,
        name="hand_on",
    )(child_factor, parent_factor, tail)
    return (
        child_factor.reshape(1, cycles, 1, CHILDREN, SUB, 1, 1, LANE),
        parent_factor.reshape(cycles, 1, 1, SUB, 1, 1, LANE),
        tail.reshape(border, 1, 1, SUB, border, 1, LANE),
    )


def solution(mesh):
    return jax.shard_map(
        shards,
        mesh=mesh,
        in_specs=(
            P("cube", None, "row", None, None, None, "col", None),
            P(None, "row", "cube", None, None, "col", None),
            P(),
        ),
        out_specs=(
            P("cube", None, "row", None, None, None, "col", None),
            P(None, "row", "cube", None, None, "col", None),
            P(None, "row", "cube", None, None, "col", None),
        ),
        check_vma=False,
    )
```
